32 devices in a mesh: shard: 8 (over z, x), context: 2 (over y), tensor: 2 (over core).
Axes of the slice: x: 2, y: 2, z: 4, core: 2. Of those that a mesh axis runs over, the one named last changes fastest.
Arguments:
- layer_input: bfloat16 [2048, 1536], P(('shard', 'context', 'tensor')), may hold values from -6 to 6
- segment_ids: int32 [8, 256], P('shard'), may hold values from 0 to 15, never falling along the last dimension, each value on 1 to 128 neighbouring positions
- routes: int32 [2048, 8], P(('shard', 'context')), may hold values from 0 to 15, all different within a row
- slot_order: int32 [16, 128], P(('shard', 'context')), may hold values from 0 to 127, each once within a row
- norm1_gain: bfloat16 [1536], P(('shard', 'context')), may hold values from 0.099609375 to 1.8984375
- norm2_gain: bfloat16 [1536], P(('shard', 'context')), may hold values from 0.099609375 to 1.8984375
- w_query: bfloat16 [1536, 1536], P(('shard', 'context'), 'tensor'), may hold values from -0.15625 to 0.15625
- w_key: bfloat16 [1536, 512], P(('shard', 'context'), 'tensor'), may hold values from -0.15625 to 0.15625
- w_value: bfloat16 [1536, 512], P(('shard', 'context'), 'tensor'), may hold values from -0.15625 to 0.15625
- w_out: bfloat16 [1536, 1536], P(('shard', 'context'), 'tensor'), may hold values from -1.25 to 1.25
- w_router: bfloat16 [1536, 16], P(('shard', 'context')), may hold values from -0.15625 to 0.15625
- w_gate: bfloat16 [16, 512, 1536], P(('shard', 'context'), 'tensor'), may hold values from -0.15625 to 0.15625
- w_up: bfloat16 [16, 512, 1536], P(('shard', 'context'), 'tensor'), may hold values from -0.15625 to 0.15625
- w_down: bfloat16 [16, 512, 1536], P(('shard', 'context'), 'tensor'), may hold values from -0.5 to 0.5
- cotangent: bfloat16 [2048, 1536], P(('shard', 'context', 'tensor')), may hold values from -6 to 6
Outputs:
- layer_output: bfloat16 [2048, 1536], P(('shard', 'context', 'tensor'))
- grad_input: float32 [2048, 1536], P(('shard', 'context', 'tensor'))
- grad_norm1: float32 [1536], P(('shard', 'context'))
- grad_norm2: float32 [1536], P(('shard', 'context'))
- grad_query: float32 [1536, 1536], P(('shard', 'context'), 'tensor')
- grad_key: float32 [1536, 512], P(('shard', 'context'), 'tensor')
- grad_value: float32 [1536, 512], P(('shard', 'context'), 'tensor')
- grad_out: float32 [1536, 1536], P(('shard', 'context'), 'tensor')
- grad_router: float32 [1536, 16], P(('shard', 'context'))
- grad_gate: float32 [16, 512, 1536], P(('shard', 'context'), 'tensor')
- grad_up: float32 [16, 512, 1536], P(('shard', 'context'), 'tensor')
- grad_down: float32 [16, 512, 1536], P(('shard', 'context'), 'tensor')
The draws below stay inside these ranges and needn't reach their ends.
Inputs may be any that keep to these rules, and one draw needn't show every extreme that they name: `routes`: each token names 8 different experts. `slot_order`: each row lists every token index of its group once. `segment_ids`: ids never fall along a sequence; a document has at most half of 256 tokens.
All inputs are finite; a program needn't handle non-finite values.
Results may differ from the reference program's by a relative error of at most 0.03.
Values may be sent and summed in bfloat16 or wider, within the bound.
No kernel may reach another device: no remote copies, remote signals or barrier semaphores. Data moves between devices by JAX's collectives and lax.ppermute only.
A program may use at most 128 MiB of HBM per device.

```python
import math
from functools import partial
import jax
import jax.numpy as jnp
import numpy as np
from jax import lax

D = 1536
HEADS = 24
KV_HEADS = 8
HEAD = 64
EXP_FF = 512
TOPK = 8
DOCS = 16
TOK_DEV = 128
SEQ_LEN = 256
N_SEQ = 8
TOKENS = 2048
GROUPS = 16
EXPERTS = 16
CAP = 80


def levels(rng, shape, cuts, smallest, high):
    loudness, own = 1.0, jax.random.fold_in(rng, 6)
    for position, blocks in cuts:
        draws = jnp.exp(jax.random.uniform(jax.random.fold_in(own, position), (blocks,), jnp.float32, smallest / len(cuts), high / len(cuts)))
        loudness = loudness * jnp.repeat(draws, shape[position] // blocks).reshape([-1 if axis == position else 1 for axis in range(len(shape))])
    return loudness


def picks_of(stream_key, rows, amount, top, lift):
    sequence = jax.random.permutation(jax.random.fold_in(stream_key, 1), amount)
    pull = sequence
    for power in range(3):
        pull = pull * pull // amount
    pull = pull * lift // amount
    lots = jax.random.randint(jax.random.fold_in(stream_key, 2), (rows, amount), 0, 4096) + pull
    sure = jax.random.permutation(jax.random.fold_in(stream_key, 3), rows)[jnp.arange(amount) % rows]
    lots = jnp.where(jnp.arange(rows)[:, None] == sure[None, :], 1 << 14, lots)
    merit = lots * amount + jnp.arange(amount)
    return lax.top_k(merit.astype(jnp.int32), top)[1].astype(jnp.int32)


def split_up(count, total, bound, lean):
    loads = [(1 << 20) // math.isqrt(grade ** lean) + 1 for grade in range(2, count + 1)]
    surplus, counts = total - bound - (count - 1), [1] * (count - 1)
    while surplus > 0:
        candidates = [i for i in range(count - 1) if counts[i] < bound]
        whole, left = sum([loads[i] for i in candidates]), surplus
        for i in candidates:
            more = min(bound - counts[i], max(1, left * loads[i] // whole), surplus)
            counts[i] = counts[i] + more
            surplus = surplus - more
    return np.array([bound] + counts)


def ragged(key, count, total, bound, slope):
    if count == 2:
        one = jax.random.randint(key, (), max(1, total - bound), min(bound, total - 1) + 1)
        return jnp.stack([one, total - one])
    sizes = jnp.asarray(split_up(count, total, bound, slope), jnp.int32)
    pairs = (count - 1) // 2
    giver, receiver = sizes[1:1 + 2 * pairs:2], sizes[2:2 + 2 * pairs:2]
    slack = jnp.minimum(giver - 1, bound - receiver)
    passed = jax.random.randint(jax.random.fold_in(key, 1), (pairs,), 0, 1 << 20) % (slack + 1)
    sizes = sizes.at[1:1 + 2 * pairs:2].set(giver - passed).at[2:2 + 2 * pairs:2].set(receiver + passed)
    return sizes[jax.random.permutation(jax.random.fold_in(key, 2), count)]


def scatter_about(stream_key, dims, spread, limit, split=(), kind=jnp.bfloat16):
    values = spread * jax.random.normal(stream_key, dims, jnp.float32)
    if split:
        values = values * levels(stream_key, dims, split, -0.22, 0.18)
    return jnp.clip(values, -limit, limit).astype(kind)


def setup_inputs(seed: int = 0) -> dict:
    streams_of = jax.random.split(jax.random.key(seed), 16)
    layer_input = scatter_about(streams_of[0], (TOKENS, D), 1.0, 6.0, ((0, 32),))
    segment_ids = jax.vmap(lambda own: jnp.searchsorted(jnp.cumsum(ragged(own, DOCS, SEQ_LEN, SEQ_LEN // 2, 2)), jnp.arange(SEQ_LEN), side="right"))(jax.random.split(streams_of[1], N_SEQ)).reshape((N_SEQ, SEQ_LEN)).astype(jnp.int32)
    routes = picks_of(streams_of[2], TOKENS, EXPERTS, TOPK, 4096)
    slot_order = jax.vmap(lambda own: jax.random.permutation(own, TOK_DEV))(jax.random.split(streams_of[3], GROUPS)).reshape((GROUPS, TOK_DEV)).astype(jnp.int32)
    norm1_gain = jnp.clip(1.0 + 0.18 * jax.random.normal(streams_of[4], (D,), jnp.float32), 0.099609375, 1.8984375).astype(jnp.bfloat16)
    norm2_gain = jnp.clip(1.0 + 0.18 * jax.random.normal(streams_of[5], (D,), jnp.float32), 0.099609375, 1.8984375).astype(jnp.bfloat16)
    w_query = scatter_about(streams_of[6], (D, HEADS * HEAD), D ** -0.5, 0.15625, ((0, 16), (1, 2)))
    w_key = scatter_about(streams_of[7], (D, KV_HEADS * HEAD), D ** -0.5, 0.15625, ((0, 16), (1, 2)))
    w_value = scatter_about(streams_of[8], (D, KV_HEADS * HEAD), D ** -0.5, 0.15625, ((0, 16), (1, 2)))
    w_out = scatter_about(streams_of[9], (D, HEADS * HEAD), (D // 64) ** -0.5, 1.25, ((0, 16), (1, 2)))
    w_router = scatter_about(streams_of[10], (D, EXPERTS), D ** -0.5, 0.15625, ((0, 16),))
    w_gate = scatter_about(streams_of[11], (EXPERTS, EXP_FF, D), D ** -0.5, 0.15625, ((0, 16), (1, 2)))
    w_up = scatter_about(streams_of[12], (EXPERTS, EXP_FF, D), D ** -0.5, 0.15625, ((0, 16), (1, 2)))
    w_down = scatter_about(streams_of[13], (EXPERTS, EXP_FF, D), (EXP_FF // 4) ** -0.5, 0.5, ((0, 16), (1, 2)))
    cotangent = scatter_about(streams_of[14], (TOKENS, D), 1.0, 6.0, ((0, 32),))
    return dict(layer_input=layer_input, segment_ids=segment_ids, routes=routes, slot_order=slot_order, norm1_gain=norm1_gain, norm2_gain=norm2_gain, w_query=w_query, w_key=w_key, w_value=w_value, w_out=w_out, w_router=w_router, w_gate=w_gate, w_up=w_up, w_down=w_down, cotangent=cotangent)


EPSILON = 1e-05
MASKED = -1e+30
HIGHEST = lax.Precision.HIGHEST

@jax.custom_vjp
def low(v):
    return lax.optimization_barrier(v.astype(jnp.bfloat16)).astype(jnp.float32)

@jax.custom_vjp
def low_back(v):
    return v

def low_keep(v):
    return (low(v), None)

def low_pass(kept, grad):
    return (grad,)

def back_keep(v):
    return (v, None)

def back_low(kept, grad):
    return (low(grad),)
low.defvjp(low_keep, low_pass)
low_back.defvjp(back_keep, back_low)

def matmul(left, right):
    return jnp.dot(left, right, precision=HIGHEST, preferred_element_type=jnp.float32)

def rms_norm(values, scale_gain):
    return values * lax.rsqrt(lax.optimization_barrier(jnp.mean(values * values, axis=-1, keepdims=True)) + EPSILON) * scale_gain

def rotary(values, positions, rotation):
    half_size = values.shape[-1] // 2
    frequency = 10000.0 ** (-jnp.arange(half_size, dtype=jnp.float32) * 2.0 / values.shape[-1])
    angles = positions.astype(jnp.float32)[:, None] * frequency[None, :]
    cosine = jnp.cos(angles)[:, None, :]
    sine_part = rotation * jnp.sin(angles)[:, None, :]
    first_half = values[..., :half_size]
    second_half = values[..., half_size:]
    return jnp.concatenate([first_half * cosine - second_half * sine_part, second_half * cosine + first_half * sine_part], axis=-1)

def slot_numbers(route_rows, priority, expert_count):
    ordered = route_rows[priority]
    flat_routes = ordered.reshape(-1)
    onehot_table = (flat_routes[:, None] == jnp.arange(expert_count, dtype=jnp.int32)[None, :]).astype(jnp.int32)
    earlier = jnp.cumsum(onehot_table, axis=0).astype(jnp.int32) - onehot_table
    ranked = lax.optimization_barrier(jnp.sum(earlier * onehot_table, axis=1)).astype(jnp.int32).reshape(ordered.shape)
    return jnp.zeros(ordered.shape, jnp.int32).at[priority].set(ranked)

def slot_tables(route_rows, priority, capacity, expert_count):
    pair_count = route_rows.shape[0] * route_rows.shape[1]
    slot_index = slot_numbers(route_rows, priority, expert_count)
    kept_mask = slot_index < capacity
    target = jnp.where(kept_mask, route_rows * capacity + slot_index, expert_count * capacity).astype(jnp.int32)
    owner_pair = jnp.full((expert_count * capacity + 1,), pair_count, jnp.int32)
    owner_pair = owner_pair.at[target.reshape(-1)].set(jnp.arange(pair_count, dtype=jnp.int32))[:-1]
    return (target, owner_pair)

def owner_table(route_rows, priority):
    return slot_tables(route_rows, priority, CAP, EXPERTS)[1]

def attend_block(keys_seq, values_seq, seg_seq, block_in):
    query_block, start = block_in
    rows_count = query_block.shape[0]
    query_pos = start + jnp.arange(rows_count, dtype=jnp.int32)
    key_pos = jnp.arange(keys_seq.shape[0], dtype=jnp.int32)
    seg_query = lax.dynamic_slice_in_dim(seg_seq, start, rows_count)
    allowed = (key_pos[None, :] <= query_pos[:, None]) & (seg_query[:, None] == seg_seq[None, :])
    scores = low_back(jnp.einsum('qhgd,khd->hgqk', query_block, keys_seq, precision=HIGHEST) * 0.125)
    scores = jnp.where(allowed[None, None], scores, MASKED)
    attn_probs = low(jax.nn.softmax(scores, axis=-1))
    return jnp.einsum('hgqk,khd->qhgd', attn_probs, values_seq, precision=HIGHEST)

def attend_sequence(seq_in):
    queries_seq, keys_seq, values_seq, seg_seq = seq_in
    block_rows = min(512, SEQ_LEN)
    block_count = SEQ_LEN // block_rows
    query_blocks = queries_seq.reshape((block_count, block_rows) + queries_seq.shape[1:])
    starts = jnp.arange(block_count, dtype=jnp.int32) * block_rows
    block_out = lax.map(jax.checkpoint(partial(attend_block, keys_seq, values_seq, seg_seq)), (query_blocks, starts))
    return block_out.reshape(queries_seq.shape)

def group_moe(gate_w, up_w, down_w, group_in):
    mixed_group, gate_group, token_group, pair_group, valid_group = group_in
    rows_in = low_back(mixed_group[token_group] * valid_group[:, None]).reshape(EXPERTS, CAP, D)
    gate_act = low_back(jnp.einsum('ecd,efd->ecf', rows_in, gate_w, precision=HIGHEST))
    up_act = low_back(jnp.einsum('ecd,efd->ecf', rows_in, up_w, precision=HIGHEST))
    inner = low(jax.nn.silu(gate_act) * up_act)
    expert_out = low_back(low(jnp.einsum('ecf,efd->ecd', inner, down_w, precision=HIGHEST))).reshape(EXPERTS * CAP, D)
    pair_weight = gate_group[pair_group] * valid_group
    return jnp.zeros((TOK_DEV, D), jnp.float32).at[token_group].add(expert_out * pair_weight[:, None])

def reference(layer_input, segment_ids, routes, slot_order, norm1_gain, norm2_gain, w_query, w_key, w_value, w_out, w_router, w_gate, w_up, w_down, cotangent):
    owners = jax.vmap(owner_table)(routes.reshape(GROUPS, TOK_DEV, TOPK), slot_order)
    pair_count = TOK_DEV * TOPK
    valid_slot = (owners < pair_count).astype(jnp.float32)
    token_slot = jnp.where(owners < pair_count, owners // TOPK, 0).astype(jnp.int32)
    pair_slot = jnp.where(owners < pair_count, owners, 0).astype(jnp.int32)
    token_pos = jnp.tile(jnp.arange(SEQ_LEN, dtype=jnp.int32), N_SEQ)
    group_size = HEADS // KV_HEADS

    def forward(inputs, gain_one, gain_two, query_w, key_w, value_w, out_w, router_w, gate_w, up_w, down_w):
        normed = low(rms_norm(inputs, gain_one))
        query_raw = low_back(matmul(normed, query_w))
        key_raw = low_back(matmul(normed, key_w))
        value_all = low_back(low(matmul(normed, value_w)))
        queries = low(rotary(query_raw.reshape(TOKENS, HEADS, HEAD), token_pos, 1.0))
        keys_all = low(rotary(key_raw.reshape(TOKENS, KV_HEADS, HEAD), token_pos, 1.0))
        attended = lax.map(attend_sequence, (queries.reshape(N_SEQ, SEQ_LEN, KV_HEADS, group_size, HEAD), keys_all.reshape(N_SEQ, SEQ_LEN, KV_HEADS, HEAD), value_all.reshape(N_SEQ, SEQ_LEN, KV_HEADS, HEAD), segment_ids))
        attended = low_back(low(attended.reshape(TOKENS, HEADS * HEAD)))
        branch = low_back(matmul(attended, out_w.T))
        hidden_state = inputs + branch
        mixed_in = low(rms_norm(hidden_state, gain_two))
        logits = low_back(matmul(mixed_in, router_w))
        picked = jnp.take_along_axis(logits, routes, axis=1)
        gate_probs = jax.nn.softmax(picked, axis=-1)
        moe_out = lax.map(jax.checkpoint(partial(group_moe, gate_w, up_w, down_w)), (mixed_in.reshape(GROUPS, TOK_DEV, D), gate_probs.reshape(GROUPS, TOK_DEV * TOPK), token_slot, pair_slot, valid_slot))
        return hidden_state + moe_out.reshape(TOKENS, D)
    primal, pullback = jax.vjp(forward, layer_input.astype(jnp.float32), norm1_gain.astype(jnp.float32), norm2_gain.astype(jnp.float32), w_query.astype(jnp.float32), w_key.astype(jnp.float32), w_value.astype(jnp.float32), w_out.astype(jnp.float32), w_router.astype(jnp.float32), w_gate.astype(jnp.float32), w_up.astype(jnp.float32), w_down.astype(jnp.float32))
    grads_all = pullback(cotangent.astype(jnp.float32))
    return (primal.astype(jnp.bfloat16), grads_all[0], grads_all[1], grads_all[2], grads_all[3], grads_all[4], grads_all[5], grads_all[6], grads_all[7], grads_all[8], grads_all[9], grads_all[10])
```

```python
import jax
import jax.numpy as jnp
from jax import lax
from jax.experimental import pallas as pl
from jax.experimental.pallas import tpu as pltpu
from jax.sharding import PartitionSpec as P

SHARD, CONTEXT, TENSOR = "shard", "context", "tensor"
CHIPS = (SHARD, CONTEXT)

HEAD = 64


EPSILON = 1e-05
MASKED = -1e30


def rotary(values, positions, rotation):
    half_size = values.shape[-1] // 2
    frequency = 10000.0 ** (-jnp.arange(half_size, dtype=jnp.float32) * 2.0 / values.shape[-1])
    angles = positions.astype(jnp.float32)[:, None] * frequency[None, :]
    cosine = jnp.cos(angles)[:, None, :]
    sine_part = rotation * jnp.sin(angles)[:, None, :]
    first_half = values[..., :half_size]
    second_half = values[..., half_size:]
    return jnp.concatenate(
        [
            first_half * cosine - second_half * sine_part,
            second_half * cosine + first_half * sine_part,
        ],
        axis=-1,
    )


def slot_numbers(route_rows, priority, expert_count):
    ordered = route_rows[priority]
    flat_routes = ordered.reshape(-1)
    onehot_table = (
        flat_routes[:, None] == jnp.arange(expert_count, dtype=jnp.int32)[None, :]
    ).astype(jnp.int32)
    earlier = jnp.cumsum(onehot_table, axis=0) - onehot_table
    ranked = jnp.sum(earlier * onehot_table, axis=1).reshape(ordered.shape)
    return jnp.zeros(ordered.shape, jnp.int32).at[priority].set(ranked)


def slot_tables(route_rows, priority, capacity, expert_count):
    pair_count = route_rows.shape[0] * route_rows.shape[1]
    slot_index = slot_numbers(route_rows, priority, expert_count)
    kept_mask = slot_index < capacity
    target = jnp.where(kept_mask, route_rows * capacity + slot_index, expert_count * capacity)
    owner_pair = jnp.full((expert_count * capacity + 1,), pair_count, jnp.int32)
    owner_pair = owner_pair.at[target.reshape(-1)].set(jnp.arange(pair_count, dtype=jnp.int32))[:-1]
    return (target, owner_pair)


def general_block(
    layer_input,
    segment_ids,
    routes,
    slot_order,
    norm1_gain,
    norm2_gain,
    w_query,
    w_key,
    w_value,
    w_out,
    w_router,
    w_gate,
    w_up,
    w_down,
    cotangent,
):
    n_tensor = lax.axis_size(TENSOR)
    tensor_index = lax.axis_index(TENSOR)
    context_index = lax.axis_index(CONTEXT)
    own_rows = layer_input.shape[0]
    tok_rows = own_rows * n_tensor
    full_width = layer_input.shape[1]
    choose_count = routes.shape[1]
    expert_count = w_router.shape[1]
    pair_count = tok_rows * choose_count
    capacity = 5 * tok_rows * choose_count // (4 * expert_count)
    cap_part = capacity // n_tensor
    slot_start = tensor_index * cap_part
    head_size = HEAD
    query_heads = w_query.shape[1] // head_size
    key_heads = w_key.shape[1] // head_size
    group_size = query_heads // key_heads
    seq_len = segment_ids.shape[1]
    block_size = min(256, seq_len)
    block_count = seq_len // block_size
    row_start = tensor_index * own_rows
    input_full, grad_full, gate_whole, up_whole, down_whole = (
        lax.all_gather(layer_input, TENSOR, axis=0, tiled=True),
        lax.all_gather(cotangent, TENSOR, axis=0, tiled=True),
        lax.all_gather(w_gate, TENSOR, axis=1, tiled=True),
        lax.all_gather(w_up, TENSOR, axis=1, tiled=True),
        lax.all_gather(w_down, TENSOR, axis=1, tiled=True),
    )
    gain_one, gain_two, query_w, key_w, value_w, out_w, router_w = (
        lax.all_gather(norm1_gain, CHIPS, axis=0, tiled=True),
        lax.all_gather(norm2_gain, CHIPS, axis=0, tiled=True),
        lax.all_gather(w_query, CHIPS, axis=0, tiled=True),
        lax.all_gather(w_key, CHIPS, axis=0, tiled=True),
        lax.all_gather(w_value, CHIPS, axis=0, tiled=True),
        lax.all_gather(w_out, CHIPS, axis=0, tiled=True),
        lax.all_gather(w_router, CHIPS, axis=0, tiled=True),
    )
    gain_one = gain_one.astype(jnp.float32)
    gain_two = gain_two.astype(jnp.float32)
    inputs = input_full.astype(jnp.float32)
    scale_one = lax.rsqrt(jnp.mean(inputs * inputs, axis=1, keepdims=True) + EPSILON)
    normed = (inputs * scale_one * gain_one).astype(jnp.bfloat16)
    query_raw = jnp.dot(normed, query_w, preferred_element_type=jnp.float32)
    key_raw = jnp.dot(normed, key_w, preferred_element_type=jnp.float32)
    value_low = jnp.dot(normed, value_w, preferred_element_type=jnp.float32).astype(jnp.bfloat16)
    positions = context_index * tok_rows + jnp.arange(tok_rows, dtype=jnp.int32)
    queries = rotary(query_raw.reshape(tok_rows, query_heads, head_size), positions, 1.0).astype(
        jnp.bfloat16
    )
    queries = queries.reshape(tok_rows, key_heads, group_size, head_size)
    keys_low = rotary(key_raw.reshape(tok_rows, key_heads, head_size), positions, 1.0).astype(
        jnp.bfloat16
    )
    keys_low = keys_low.reshape(tok_rows, key_heads * head_size)
    keys_all, values_all = (
        lax.all_gather(keys_low, CONTEXT, axis=0, tiled=True),
        lax.all_gather(value_low, CONTEXT, axis=0, tiled=True),
    )
    seg_row = segment_ids[0]
    seg_query = lax.dynamic_slice_in_dim(seg_row, context_index * tok_rows, tok_rows)
    key_blocks = keys_all.reshape(block_count, block_size, key_heads, head_size)
    value_blocks = values_all.reshape(block_count, block_size, key_heads, head_size)
    seg_blocks = seg_row.reshape(block_count, block_size)
    block_starts = jnp.arange(block_count, dtype=jnp.int32) * block_size
    block_inputs = (key_blocks, value_blocks, block_starts, seg_blocks)

    def block_scores(key_block, key_start, seg_block):
        raw_scores = (
            jnp.einsum("qhgd,khd->hgqk", queries, key_block, preferred_element_type=jnp.float32)
            * 0.125
        )
        key_pos = key_start + jnp.arange(key_block.shape[0], dtype=jnp.int32)
        allowed = (key_pos[None, :] <= positions[:, None]) & (
            seg_block[None, :] == seg_query[:, None]
        )
        return (raw_scores, allowed[None, None])

    def running_max(running, block_in):
        row_max, row_sum = running
        key_block, value_block, key_start, seg_block = block_in
        raw_scores, allowed = block_scores(key_block, key_start, seg_block)
        new_max = jnp.maximum(row_max, jnp.max(jnp.where(allowed, raw_scores, MASKED), axis=-1))
        terms = jnp.where(allowed, jnp.exp(raw_scores - new_max[..., None]), 0.0)
        row_sum = row_sum * jnp.exp(row_max - new_max) + jnp.sum(terms, axis=-1)
        return ((new_max, row_sum), None)

    start_max = jnp.full((key_heads, group_size, tok_rows), MASKED, jnp.float32)
    start_sum = jnp.zeros((key_heads, group_size, tok_rows), jnp.float32)
    (row_max, row_sum), unused = lax.scan(running_max, (start_max, start_sum), block_inputs)
    log_total = row_max + jnp.log(row_sum)

    def attend_step(accum, block_in):
        key_block, value_block, key_start, seg_block = block_in
        raw_scores, allowed = block_scores(key_block, key_start, seg_block)
        probs_low = jnp.where(allowed, jnp.exp(raw_scores - log_total[..., None]), 0.0).astype(
            jnp.bfloat16
        )
        accum = accum + jnp.einsum(
            "hgqk,khd->qhgd", probs_low, value_block, preferred_element_type=jnp.float32
        )
        return (accum, None)

    attn_start = jnp.zeros((tok_rows, key_heads, group_size, head_size), jnp.float32)
    attended_f, unused = lax.scan(attend_step, attn_start, block_inputs)
    attended = attended_f.astype(jnp.bfloat16).reshape(tok_rows, query_heads * head_size)
    branch_part = lax.dot_general(
        attended, out_w, (((1,), (1,)), ((), ())), preferred_element_type=jnp.float32
    )
    branch = lax.psum(branch_part.astype(jnp.bfloat16), TENSOR).astype(jnp.float32)
    hidden_state = inputs + branch
    scale_two = lax.rsqrt(jnp.mean(hidden_state * hidden_state, axis=1, keepdims=True) + EPSILON)
    mixed_in = (hidden_state * scale_two * gain_two).astype(jnp.bfloat16)
    logits = jnp.dot(mixed_in, router_w, preferred_element_type=jnp.float32)
    route_onehot = routes[:, :, None] == jnp.arange(expert_count, dtype=jnp.int32)[None, None, :]
    picked = jnp.sum(jnp.where(route_onehot, logits[:, None, :], 0.0), axis=-1)
    gate_probs = jax.nn.softmax(picked, axis=-1)
    target, owner_pair = slot_tables(routes, slot_order[0], capacity, expert_count)
    owner_local = lax.dynamic_slice_in_dim(
        owner_pair.reshape(expert_count, capacity), slot_start, cap_part, 1
    )
    token_local = owner_local // choose_count
    flat_owner = owner_local.reshape(-1)
    flat_token = token_local.reshape(-1)
    mixed_pad = jnp.concatenate([mixed_in, jnp.zeros((1, full_width), jnp.bfloat16)], axis=0)
    send_rows = mixed_pad[token_local]
    rows_in = lax.all_to_all(
        send_rows, CHIPS, split_axis=0, concat_axis=1, tiled=True
    )
    gate_act = jnp.einsum("erd,efd->erf", rows_in, gate_whole, preferred_element_type=jnp.float32)
    up_act = jnp.einsum("erd,efd->erf", rows_in, up_whole, preferred_element_type=jnp.float32)
    inner_low = (jax.nn.silu(gate_act) * up_act).astype(jnp.bfloat16)
    expert_low = jnp.einsum(
        "erf,efd->erd", inner_low, down_whole, preferred_element_type=jnp.float32
    ).astype(jnp.bfloat16)
    returned = lax.all_to_all(
        expert_low, CHIPS, split_axis=1, concat_axis=0, tiled=True
    )
    gate_pad = jnp.concatenate([gate_probs.reshape(-1), jnp.zeros((1,), jnp.float32)], axis=0)
    gate_local = gate_pad[owner_local]
    grad_pad = jnp.concatenate([grad_full, jnp.zeros((1, full_width), jnp.bfloat16)], axis=0)
    dy_rows = grad_pad[token_local].astype(jnp.float32)
    returned_f = returned.astype(jnp.float32)
    dgate_slot = jnp.sum(returned_f * dy_rows, axis=2)
    dgate_part = (
        jnp.zeros((pair_count + 1,), jnp.float32)
        .at[flat_owner]
        .add(dgate_slot.reshape(-1))[:pair_count]
    )
    dgate_part = dgate_part.reshape(tok_rows, choose_count)
    all_slots = lax.all_gather(returned, TENSOR, axis=1, tiled=True)
    slots_pad = jnp.concatenate(
        [
            all_slots.reshape(expert_count * capacity, full_width),
            jnp.zeros((1, full_width), jnp.bfloat16),
        ],
        axis=0,
    )
    own_target = lax.dynamic_slice_in_dim(target, row_start, own_rows, 0)
    own_gate = lax.dynamic_slice_in_dim(gate_probs, row_start, own_rows, 0)
    own_picked = (
        slots_pad[own_target.reshape(-1)]
        .reshape(own_rows, choose_count, full_width)
        .astype(jnp.float32)
    )
    mixture_own = jnp.sum(own_picked * own_gate[:, :, None], axis=1)
    hidden_own = lax.dynamic_slice_in_dim(hidden_state, row_start, own_rows, 0)
    layer_output = (hidden_own + mixture_own).astype(jnp.bfloat16)
    grad_outer = grad_full.astype(jnp.float32)
    grad_send = (dy_rows * gate_local[:, :, None]).astype(jnp.bfloat16)
    grad_rows = lax.all_to_all(
        grad_send, CHIPS, split_axis=0, concat_axis=1, tiled=True
    )
    grad_inner = jnp.einsum(
        "erd,efd->erf", grad_rows, down_whole, preferred_element_type=jnp.float32
    )
    down_grad = jnp.einsum("erf,erd->efd", inner_low, grad_rows, preferred_element_type=jnp.float32)
    sigmoid_gate = jax.nn.sigmoid(gate_act)
    grad_gate_act = (
        grad_inner * up_act * sigmoid_gate * (1.0 + gate_act * (1.0 - sigmoid_gate))
    ).astype(jnp.bfloat16)
    grad_up_act = (grad_inner * gate_act * sigmoid_gate).astype(jnp.bfloat16)
    gate_grad = jnp.einsum(
        "erf,erd->efd", grad_gate_act, rows_in, preferred_element_type=jnp.float32
    )
    up_grad = jnp.einsum("erf,erd->efd", grad_up_act, rows_in, preferred_element_type=jnp.float32)
    rows_back = jnp.einsum(
        "erf,efd->erd", grad_gate_act, gate_whole, preferred_element_type=jnp.float32
    )
    rows_back = rows_back + jnp.einsum(
        "erf,efd->erd", grad_up_act, up_whole, preferred_element_type=jnp.float32
    )
    back_rows = lax.all_to_all(
        rows_back.astype(jnp.bfloat16),
        CHIPS,
        split_axis=1,
        concat_axis=0,
        tiled=True,
    )
    dmixed_part = (
        jnp.zeros((tok_rows + 1, full_width), jnp.float32)
        .at[flat_token]
        .add(back_rows.astype(jnp.float32).reshape(-1, full_width))[:tok_rows]
    )
    dmixed_experts, dgate = (
        lax.psum(dmixed_part.astype(jnp.bfloat16), TENSOR).astype(jnp.float32),
        lax.psum(dgate_part.astype(jnp.bfloat16), TENSOR).astype(jnp.float32),
    )
    dpicked = gate_probs * (dgate - jnp.sum(gate_probs * dgate, axis=1, keepdims=True))
    dlogits = jnp.sum(jnp.where(route_onehot, dpicked[:, :, None], 0.0), axis=1).astype(
        jnp.bfloat16
    )
    drouter = lax.dot_general(
        mixed_in, dlogits, (((0,), (0,)), ((), ())), preferred_element_type=jnp.float32
    )
    dmixed = dmixed_experts + lax.dot_general(
        dlogits, router_w, (((1,), (1,)), ((), ())), preferred_element_type=jnp.float32
    )
    dgain_two = jnp.sum(dmixed * hidden_state * scale_two, axis=0)
    inner_two = jnp.sum(dmixed * gain_two * hidden_state, axis=1, keepdims=True) / full_width
    dhidden = grad_outer + dmixed * gain_two * scale_two - hidden_state * scale_two**3 * inner_two
    dbranch = dhidden.astype(jnp.bfloat16)
    dout_w = lax.dot_general(
        dbranch, attended, (((0,), (0,)), ((), ())), preferred_element_type=jnp.float32
    )
    dattended = jnp.dot(dbranch, out_w, preferred_element_type=jnp.float32).astype(jnp.bfloat16)
    dattended = dattended.reshape(tok_rows, key_heads, group_size, head_size)
    row_delta = jnp.einsum("qhgd,qhgd->hgq", dattended.astype(jnp.float32), attended_f)

    def backward_step(dquery_acc, block_in):
        key_block, value_block, key_start, seg_block = block_in
        raw_scores, allowed = block_scores(key_block, key_start, seg_block)
        attn_probs = jnp.where(allowed, jnp.exp(raw_scores - log_total[..., None]), 0.0)
        probs_low = attn_probs.astype(jnp.bfloat16)
        dprobs = jnp.einsum(
            "qhgd,khd->hgqk", dattended, value_block, preferred_element_type=jnp.float32
        )
        dscores = (attn_probs * (dprobs - row_delta[..., None])).astype(jnp.bfloat16)
        dquery_acc = dquery_acc + jnp.einsum(
            "hgqk,khd->qhgd", dscores, key_block, preferred_element_type=jnp.float32
        )
        dkey_block = (
            jnp.einsum("hgqk,qhgd->khd", dscores, queries, preferred_element_type=jnp.float32)
            * 0.125
        )
        dvalue_block = jnp.einsum(
            "hgqk,qhgd->khd", probs_low, dattended, preferred_element_type=jnp.float32
        )
        return (dquery_acc, (dkey_block, dvalue_block))

    dquery_acc, (dkey_blocks, dvalue_blocks) = lax.scan(backward_step, attn_start, block_inputs)
    dkeys_seq = dkey_blocks.reshape(seq_len, key_heads * head_size)
    dvalues_seq = dvalue_blocks.reshape(seq_len, key_heads * head_size)
    dkeys, dvalues = (
        lax.psum_scatter(
            dkeys_seq.astype(jnp.bfloat16), CONTEXT, scatter_dimension=0, tiled=True
        ).astype(jnp.float32),
        lax.psum_scatter(
            dvalues_seq.astype(jnp.bfloat16), CONTEXT, scatter_dimension=0, tiled=True
        ).astype(jnp.float32),
    )
    dquery_raw = rotary(
        (dquery_acc * 0.125).reshape(tok_rows, query_heads, head_size), positions, -1.0
    )
    dquery_raw = dquery_raw.astype(jnp.bfloat16).reshape(tok_rows, query_heads * head_size)
    dkey_raw = rotary(dkeys.reshape(tok_rows, key_heads, head_size), positions, -1.0)
    dkey_raw = dkey_raw.astype(jnp.bfloat16).reshape(tok_rows, key_heads * head_size)
    dvalue_low = dvalues.astype(jnp.bfloat16)
    contract_rows = (((0,), (0,)), ((), ()))
    contract_cols = (((1,), (1,)), ((), ()))
    dquery_w = lax.dot_general(
        normed, dquery_raw, contract_rows, preferred_element_type=jnp.float32
    )
    dkey_w = lax.dot_general(normed, dkey_raw, contract_rows, preferred_element_type=jnp.float32)
    dvalue_w = lax.dot_general(
        normed, dvalue_low, contract_rows, preferred_element_type=jnp.float32
    )
    dnormed_part = lax.dot_general(
        dquery_raw, query_w, contract_cols, preferred_element_type=jnp.float32
    )
    dnormed_part = dnormed_part + lax.dot_general(
        dkey_raw, key_w, contract_cols, preferred_element_type=jnp.float32
    )
    dnormed_part = dnormed_part + lax.dot_general(
        dvalue_low, value_w, contract_cols, preferred_element_type=jnp.float32
    )
    dnormed = lax.psum(dnormed_part.astype(jnp.bfloat16), TENSOR).astype(jnp.float32)
    dgain_one = jnp.sum(dnormed * inputs * scale_one, axis=0)
    inner_one = jnp.sum(dnormed * gain_one * inputs, axis=1, keepdims=True) / full_width
    dinput = dhidden + dnormed * gain_one * scale_one - inputs * scale_one**3 * inner_one
    grad_input = lax.dynamic_slice_in_dim(dinput, row_start, own_rows, 0)
    grad_gate, grad_up, grad_down = (
        lax.psum_scatter(
            gate_grad.astype(jnp.bfloat16), TENSOR, scatter_dimension=1, tiled=True
        ).astype(jnp.float32),
        lax.psum_scatter(
            up_grad.astype(jnp.bfloat16), TENSOR, scatter_dimension=1, tiled=True
        ).astype(jnp.float32),
        lax.psum_scatter(
            down_grad.astype(jnp.bfloat16), TENSOR, scatter_dimension=1, tiled=True
        ).astype(jnp.float32),
    )
    grad_norm1, grad_norm2, grad_query, grad_key, grad_value, grad_out, grad_router = (
        lax.psum_scatter(
            dgain_one.astype(jnp.bfloat16), CHIPS, scatter_dimension=0, tiled=True
        ).astype(jnp.float32),
        lax.psum_scatter(
            dgain_two.astype(jnp.bfloat16), CHIPS, scatter_dimension=0, tiled=True
        ).astype(jnp.float32),
        lax.psum_scatter(
            dquery_w.astype(jnp.bfloat16), CHIPS, scatter_dimension=0, tiled=True
        ).astype(jnp.float32),
        lax.psum_scatter(
            dkey_w.astype(jnp.bfloat16), CHIPS, scatter_dimension=0, tiled=True
        ).astype(jnp.float32),
        lax.psum_scatter(
            dvalue_w.astype(jnp.bfloat16), CHIPS, scatter_dimension=0, tiled=True
        ).astype(jnp.float32),
        lax.psum_scatter(
            dout_w.astype(jnp.bfloat16), CHIPS, scatter_dimension=0, tiled=True
        ).astype(jnp.float32),
        lax.psum_scatter(
            drouter.astype(jnp.bfloat16), CHIPS, scatter_dimension=0, tiled=True
        ).astype(jnp.float32),
    )
    return (
        layer_output,
        grad_input,
        grad_norm1,
        grad_norm2,
        grad_query,
        grad_key,
        grad_value,
        grad_out,
        grad_router,
        grad_gate,
        grad_up,
        grad_down,
    )


LINE, PAIR = 4, 2
LANES = 128
ROWS = ((0,), (0,))
COLS = ((1,), (1,))
PLAIN = ((1,), (0,))
LOW, FULL = jnp.bfloat16, jnp.float32


def shift(block, dz=0, dx=0, dy=0):
    pairs = []
    for z in range(LINE):
        for x in range(PAIR):
            for y in range(PAIR):
                target = (((z ^ dz) * PAIR + (x ^ dx)) * PAIR) + (y ^ dy)
                pairs.append(((z * PAIR + x) * PAIR + y, target))
    return lax.ppermute(block, CHIPS, pairs)


def swap_core(block):
    return lax.ppermute(block, TENSOR, [(0, 1), (1, 0)])


def plane(block):
    return [shift(block, dy=1), shift(block, dx=1), shift(block, dx=1, dy=1)]


def dot(left, right, dims):
    return lax.dot_general(left, right, (dims, ((), ())), preferred_element_type=FULL)


def unscramble(parts, x_index, y_index):
    def pick(bit, first, second):
        return jnp.where(bit == 0, first, second)

    a, b, c, d = parts
    a, b, c, d = (
        pick(y_index, a, b),
        pick(y_index, b, a),
        pick(y_index, c, d),
        pick(y_index, d, c),
    )
    return [
        pick(x_index, a, c),
        pick(x_index, b, d),
        pick(x_index, c, a),
        pick(x_index, d, b),
    ]


def kernel_call(body, outs, *operands, scratch=()):
    specs = [pl.BlockSpec(memory_space=pltpu.SMEM)]
    specs += [pl.BlockSpec(memory_space=pltpu.VMEM) for _ in operands[1:]]
    return pl.pallas_call(
        body,
        out_shape=[jax.ShapeDtypeStruct(shape, kind) for shape, kind in outs],
        in_specs=specs,
        out_specs=[pl.BlockSpec(memory_space=pltpu.VMEM) for _ in outs],
        scratch_shapes=list(scratch),
        compiler_params=pltpu.CompilerParams(vmem_limit_bytes=56 * 1024 * 1024),
    )(*operands)


def line_slice(place, step, size):
    return pl.ds(pl.multiple_of((place[0] ^ step) * size, LANES), size)


def half_turn(values):
    width = values.shape[1]
    lane = lax.broadcasted_iota(jnp.int32, values.shape, 1)
    up = pltpu.roll(values, width - HEAD // 2, 1)
    down = pltpu.roll(values, HEAD // 2, 1)
    return jnp.where(lane % HEAD < HEAD // 2, up, down)


def twice(table):
    return jnp.concatenate([table, table], axis=0)


def join_tokens(near, far):
    count = near.shape[0] // 2
    return jnp.concatenate([near[:count], far[:count], near[count:], far[count:]], axis=0)


def split_tokens(values):
    count = values.shape[0] // 4
    near = jnp.concatenate([values[:count], values[2 * count : 3 * count]], axis=0)
    far = jnp.concatenate([values[count : 2 * count], values[3 * count :]], axis=0)
    return near, far


def attend_body(
    place, near, far, w0, w1, w2, w3, cosine, sine, pos_col, pos_row, seg_col, seg_row,
    normed_out, scale_out, qkv_out, attended_out, probs_out, tail_out,
):
    weights = (w0, w1, w2, w3)
    size = w0.shape[0]
    for step, weight in enumerate(weights):
        turned = weight[:, 2 * LANES :].astype(FULL).T
        tail_out[:, line_slice(place, step, size)] = turned[HEAD : HEAD + 32]
    inputs = join_tokens(near[...], far[...]).astype(FULL)
    scale = lax.rsqrt(jnp.mean(inputs * inputs, axis=1, keepdims=True) + EPSILON)
    scale_out[...] = scale
    normed_out[...] = (inputs * scale * tail_out[16:17, :]).astype(LOW)
    raw = 0.0
    for step, weight in enumerate(weights):
        raw = raw + dot(normed_out[:, line_slice(place, step, size)], weight[...], PLAIN)
    turned = raw * twice(cosine[...]) + half_turn(raw) * twice(sine[...])
    qkv_out[...] = turned.astype(LOW)
    length = raw.shape[0] // 2
    for seq in range(2):
        span = slice(seq * length, (seq + 1) * length)
        allowed = (pos_row[...] <= pos_col[...]) & (seg_row[seq : seq + 1] == seg_col[span])
        keys = qkv_out[span, 3 * HEAD : 4 * HEAD]
        values = qkv_out[span, 4 * HEAD : 5 * HEAD]
        heads = []
        for head in range(3):
            queries = qkv_out[span, head * HEAD : (head + 1) * HEAD]
            scores = jnp.where(allowed, dot(queries, keys, COLS) * 0.125, MASKED)
            top = jnp.max(scores, axis=1, keepdims=True)
            terms = jnp.where(allowed, jnp.exp(scores - top), 0.0)
            probs = terms / jnp.sum(terms, axis=1, keepdims=True)
            probs_out[seq * 3 + head] = probs
            heads.append(dot(probs.astype(LOW), values, PLAIN))
        attended_out[span] = jnp.concatenate(heads, axis=1).astype(LOW)


def branch_body(place, attended, o0, o1, o2, o3, near_out, far_out):
    for step, weight in enumerate((o0, o1, o2, o3)):
        near, far = split_tokens(dot(attended[...], weight[...], COLS))
        span = line_slice(place, step, weight.shape[0])
        near_out[:, span] = near
        far_out[:, span] = far.astype(LOW)


def two_parts(value):
    high = value.astype(LOW)
    return high, (value - high.astype(FULL)).astype(LOW)


def router_body(
    place, inputs, mine, r1, r2, r3, tail, chosen, kept,
    hidden_out, mixed_out, gates_out, scale_out,
):
    hidden = inputs[...].astype(FULL) + mine[...].astype(FULL)
    hidden = hidden + r1[...].astype(FULL) + r2[...].astype(FULL) + r3[...].astype(FULL)
    hidden_out[...] = hidden
    scale = lax.rsqrt(jnp.mean(hidden * hidden, axis=1, keepdims=True) + EPSILON)
    scale_out[...] = scale
    mixed = (hidden * scale * tail[17:18, :]).astype(LOW)
    width = mixed.shape[1]
    mixed_out[:, :width] = mixed
    logits = dot(mixed, tail[...].astype(LOW), COLS)
    on = chosen[...] > 0.0
    best = jnp.max(jnp.where(on, logits, MASKED), axis=1, keepdims=True)
    gates = jnp.where(on, jnp.exp(logits - best), 0.0)
    gates = gates / jnp.sum(gates, axis=1, keepdims=True)
    gates_out[...] = gates
    high, rest = two_parts(gates * kept[...])
    blank = jnp.zeros((mixed.shape[0], LANES - 64), LOW)
    mixed_out[:, width:] = jnp.concatenate([high, rest, blank], axis=1)


def upstream_body(place, d0, d1, d2, d3, own_w, far_w, plain0, plain1, dy0, dy1):
    for chunk, ref in enumerate((d0, d1, d2, d3)):
        value = ref[...]
        flat = jnp.concatenate([dot(value, own_w[...], COLS), dot(value, far_w[...], COLS)], axis=1)
        for block in range(4):
            for batch, (plain, copy) in enumerate(((plain0, dy0), (plain1, dy1))):
                source = slice(block * 64 + batch * 32, block * 64 + batch * 32 + 32)
                target = slice(chunk * 128 + block * 32, chunk * 128 + block * 32 + 32)
                plain[target] = flat[source]
                copy[target] = value[source]


def expert_body(
    place, c0, c1, c2, c3, plain, gate_own, gate_far, up_own, up_far,
    b0, b1, b2, b3, inner_out, d_gate_out, d_up_out,
):
    width = gate_own.shape[1]
    part = gate_own.shape[0]
    for chunks, backs, start in (((c0, c1), (b0, b1), 0), ((c2, c3), (b2, b3), 256)):
        rows = jnp.concatenate([ref[:, :width] for ref in chunks], axis=0)
        tails = jnp.concatenate([ref[:, width:] for ref in chunks], axis=0).astype(FULL)
        span = slice(start, start + 256)
        lane = lax.broadcasted_iota(jnp.int32, tails.shape, 1)
        is_top, is_rest = lane == place[1], lane == place[1] + 32
        gate = jnp.sum(jnp.where(is_top | is_rest, tails, 0.0), axis=1, keepdims=True)
        d_gate = 0.0
        d_rows = 0.0
        for half, (gate_w, up_w) in enumerate(((gate_own, up_own), (gate_far, up_far))):
            cols = slice(half * part, (half + 1) * part)
            gate_act = dot(rows, gate_w[...], COLS)
            up_act = dot(rows, up_w[...], COLS)
            sig = 1.0 / (1.0 + jnp.exp(-gate_act))
            silu = gate_act * sig
            inner = silu * up_act
            d_plain = plain[span, cols]
            d_gate = d_gate + jnp.sum(inner * d_plain, axis=1, keepdims=True)
            inner_out[span, cols] = (inner * gate).astype(LOW)
            d_inner = d_plain * gate
            d_gate_act = (d_inner * up_act * sig * (1.0 + gate_act * (1.0 - sig))).astype(LOW)
            d_up_act = (d_inner * silu).astype(LOW)
            d_gate_out[span, cols] = d_gate_act
            d_up_out[span, cols] = d_up_act
            d_rows = d_rows + dot(d_gate_act, gate_w[...], PLAIN)
            d_rows = d_rows + dot(d_up_act, up_w[...], PLAIN)
        high, rest = two_parts(d_gate)
        zero = jnp.zeros((), FULL)
        tail = jnp.where(is_top, high.astype(FULL), jnp.where(is_rest, rest.astype(FULL), zero))
        for at, back in enumerate(backs):
            rows_at = slice(at * 128, at * 128 + 128)
            back[:, :width] = d_rows[rows_at].astype(LOW)
            back[:, width:] = tail[rows_at].astype(LOW)


def output_body(place, inner0, inner1, own_w, far_w, o0, o1, o2, o3):
    part = own_w.shape[0]
    for batch, inner in enumerate((inner0, inner1)):
        for chunk, out in enumerate((o0, o1, o2, o3)):
            value = inner[chunk * 128 : chunk * 128 + 128]
            rows = dot(value[:, :part], own_w[...], PLAIN) + dot(value[:, part:], far_w[...], PLAIN)
            for block in range(4):
                target = slice(block * 64 + batch * 32, block * 64 + batch * 32 + 32)
                out[target] = rows[block * 32 : block * 32 + 32].astype(LOW)


def weight_body(
    place, c0, c1, c2, c3, c4, c5, c6, c7, dy0, dy1, inner0, inner1, g0, g1, u0, u1,
    mine_out, send_out,
):
    width = dy0.shape[1]
    part = mine_out.shape[1]
    rows = [
        jnp.concatenate([ref[:, :width] for ref in group], axis=0)
        for group in ((c0, c1, c2, c3), (c4, c5, c6, c7))
    ]
    for which, (left0, left1, right) in enumerate(
        ((g0, g1, rows), (u0, u1, rows), (inner0, inner1, (dy0[...], dy1[...])))
    ):
        for half in range(2):
            cols = slice(half * part, (half + 1) * part)
            total = dot(left0[:, cols], right[0], ROWS) + dot(left1[:, cols], right[1], ROWS)
            if half == 0:
                mine_out[which] = total
            else:
                send_out[which] = total.astype(LOW)


def middle_body(
    place, a0, a1, a2, a3, b0, b1, b2, b3, tail, gates, kept, hidden_in, mixed, scale_in, grad,
    d_hidden_out, d_branch_out, d_tail_out,
):
    def total(refs):
        value = refs[0][...].astype(FULL)
        for ref in refs[1:]:
            value = value + ref[...].astype(FULL)
        return value

    back = jnp.concatenate([total((a0, a1, a2, a3)), total((b0, b1, b2, b3))], axis=0)
    width = grad.shape[1]
    d_gates = (back[:, width : width + 32] + back[:, width + 32 : width + 64]) * kept[...]
    gate = gates[...]
    d_logits = gate * (d_gates - jnp.sum(gate * d_gates, axis=1, keepdims=True))
    d_logits = d_logits.astype(LOW)
    d_router = dot(d_logits, mixed[:, :width], ROWS)
    d_mixed = back[:, :width] + dot(d_logits, tail[...].astype(LOW), PLAIN)
    hidden, scale, gain = hidden_in[...], scale_in[...], tail[17:18, :]
    d_gain = jnp.sum(d_mixed * hidden * scale, axis=0, keepdims=True)
    row = lax.broadcasted_iota(jnp.int32, d_router.shape, 0)
    d_tail_out[...] = jnp.where(row == 17, d_gain, d_router)
    scaled = d_mixed * gain
    inner = jnp.sum(scaled * hidden, axis=1, keepdims=True) / width
    d_hidden = grad[...].astype(FULL) + scaled * scale - hidden * (scale * scale * scale) * inner
    d_hidden_out[...] = d_hidden
    d_branch_out[...] = d_hidden.astype(LOW)


def backward_body(
    place, near, far, o0, o1, o2, o3, attended, probs_in, qkv, cosine, sine,
    d_raw_out, e0, e1, e2, e3, d_branch, d_turned,
):
    d_branch[...] = join_tokens(near[...], far[...])
    size = o0.shape[0]
    d_attended = 0.0
    for step, (weight, out) in enumerate(((o0, e0), (o1, e1), (o2, e2), (o3, e3))):
        piece = d_branch[:, line_slice(place, step, size)]
        d_attended = d_attended + dot(piece, weight[...], PLAIN)
        out[...] = dot(piece, attended[...], ROWS).astype(out.dtype)
    d_attended = d_attended.astype(LOW)
    length = d_attended.shape[0] // 2
    for seq in range(2):
        span = slice(seq * length, (seq + 1) * length)
        keys = qkv[span, 3 * HEAD : 4 * HEAD]
        values = qkv[span, 4 * HEAD : 5 * HEAD]
        pieces, d_keys, d_values = [], 0.0, 0.0
        for head in range(3):
            queries = qkv[span, head * HEAD : (head + 1) * HEAD]
            d_head = d_attended[span, head * HEAD : (head + 1) * HEAD]
            probs = probs_in[seq * 3 + head]
            d_probs = dot(d_head, values, COLS)
            delta = jnp.sum(probs * d_probs, axis=1, keepdims=True)
            d_scores = (probs * (d_probs - delta)).astype(LOW)
            pieces.append(dot(d_scores, keys, PLAIN) * 0.125)
            d_keys = d_keys + dot(d_scores, queries, ROWS) * 0.125
            d_values = d_values + dot(probs.astype(LOW), d_head, ROWS)
        blank = jnp.zeros((length, HEAD), FULL)
        d_turned[span] = jnp.concatenate([*pieces, d_keys, d_values, blank], axis=1)
    value = d_turned[...]
    turned = value * twice(cosine[...]) - half_turn(value) * twice(sine[...])
    d_raw_out[...] = turned.astype(LOW)


def project_body(
    place, d_raw, normed, near, far, scale, w0, w1, w2, w3, d_tail,
    near_out, far_out, e0, e1, e2, e3,
):
    size = w0.shape[0]
    d_value = d_raw[...]
    for step, (weight, out) in enumerate(((w0, e0), (w1, e1), (w2, e2), (w3, e3))):
        span = line_slice(place, step, size)
        d_normed = dot(d_value, weight[...], COLS)
        inputs = join_tokens(near[:, span], far[:, span]).astype(FULL)
        d_gain = jnp.sum(d_normed * inputs * scale[...], axis=0, keepdims=True)
        d_near, d_far = split_tokens(d_normed)
        near_out[:, span] = d_near
        far_out[:, span] = d_far.astype(LOW)
        tail = d_tail[:, span]
        row = lax.broadcasted_iota(jnp.int32, tail.shape, 0)
        tail = jnp.where(row == 16, d_gain, tail)
        pad = jnp.zeros((HEAD, size), FULL)
        tail = jnp.concatenate([pad, tail, pad[:32]], axis=0).T
        d_weight = dot(normed[:, span], d_value, ROWS)
        out[:, : 2 * LANES] = d_weight[:, : 2 * LANES].astype(out.dtype)
        out[:, 2 * LANES :] = (d_weight[:, 2 * LANES :] + tail).astype(out.dtype)


def final_body(place, mine, r1, r2, r3, inputs_in, tail, d_hidden, out):
    d_normed = mine[...].astype(FULL) + r1[...].astype(FULL)
    d_normed = d_normed + r2[...].astype(FULL) + r3[...].astype(FULL)
    inputs = inputs_in[...].astype(FULL)
    width = inputs.shape[1]
    scale = lax.rsqrt(jnp.mean(inputs * inputs, axis=1, keepdims=True) + EPSILON)
    scaled = d_normed * tail[16:17, :]
    inner = jnp.sum(scaled * inputs, axis=1, keepdims=True) / width
    out[...] = d_hidden[...] + scaled * scale - inputs * (scale * scale * scale) * inner


def spread(block):
    line = [block] + [shift(block, dz=step) for step in range(1, LINE)]
    first = jnp.concatenate(line[:2], axis=0)
    second = jnp.concatenate(line[2:], axis=0)
    first = jnp.concatenate([first, shift(first, dx=1)], axis=0)
    second = jnp.concatenate([second, shift(second, dy=1)], axis=0)
    return [first, shift(first, dy=1), second, shift(second, dx=1)]


def add_low(left, right):
    return (left.astype(FULL) + right.astype(FULL)).astype(LOW)


def collect(chunks):
    first = add_low(chunks[0], shift(chunks[1], dy=1))
    second = add_low(chunks[2], shift(chunks[3], dx=1))
    half = first.shape[0] // 2
    first = add_low(first[:half], shift(first[half:], dx=1))
    second = add_low(second[:half], shift(second[half:], dy=1))
    half = half // 2
    return [
        first[:half],
        shift(first[half:], dz=1),
        shift(second[:half], dz=2),
        shift(second[half:], dz=3),
    ]


def fast_block(
    layer_input,
    segment_ids,
    routes,
    slot_order,
    norm1_gain,
    norm2_gain,
    w_query,
    w_key,
    w_value,
    w_out,
    w_router,
    w_gate,
    w_up,
    w_down,
    cotangent,
):
    shard_index = lax.axis_index(SHARD)
    core = lax.axis_index(TENSOR)
    y_index = lax.axis_index(CONTEXT)
    z_index, x_index = shard_index // PAIR, shard_index % PAIR
    mine = x_index * PAIR + y_index
    own, width = layer_input.shape
    group = own * 2
    seq_len = segment_ids.shape[1]
    features = w_query.shape[0]
    choose = routes.shape[1]
    experts = w_router.shape[1]
    capacity = 5 * group * choose // (4 * experts)
    place = jnp.stack([z_index, shard_index * PAIR + y_index]).astype(jnp.int32)

    q_cols, k_cols = w_query.shape[1] // 4, w_key.shape[1] // 4
    extra = jnp.concatenate(
        [
            w_router,
            norm1_gain[:, None],
            norm2_gain[:, None],
            jnp.zeros((features, HEAD - 2 - experts), LOW),
        ],
        axis=1,
    )
    pack = jnp.concatenate(
        [
            w_query.reshape(features, 4, q_cols),
            w_key.reshape(features, 4, k_cols),
            w_value.reshape(features, 4, k_cols),
            jnp.broadcast_to(extra[:, None], (features, 4, HEAD)),
            w_out.reshape(features, 4, q_cols),
        ],
        axis=2,
    ).transpose(1, 0, 2)

    def eighth(step):
        return lax.dynamic_index_in_dim(pack, mine ^ step, 0, keepdims=False)

    parts = [
        eighth(0),
        shift(eighth(1), dy=1),
        shift(eighth(2), dx=1),
        shift(eighth(3), dx=1, dy=1),
    ]
    rows = jnp.concatenate(unscramble(parts, x_index, y_index), axis=0)
    a_cols = q_cols + 2 * k_cols + HEAD
    a_rows, b_rows = rows[:, :a_cols], rows[:, a_cols:]
    a_line = [a_rows] + [shift(a_rows, dz=step) for step in range(1, LINE)]

    def gather_tokens(block):
        near = jnp.concatenate([block, *plane(block)], axis=0)
        return near, swap_core(near)

    near_in, far_in = gather_tokens(layer_input)
    b_line = [b_rows] + [shift(b_rows, dz=step) for step in range(1, LINE)]

    def reduce_tokens(near, far):
        total = (near + swap_core(far).astype(FULL)).astype(LOW)
        blocks = [total[n * own : (n + 1) * own] for n in range(4)]
        return [
            blocks[0],
            shift(blocks[1], dy=1),
            shift(blocks[2], dx=1),
            shift(blocks[3], dx=1, dy=1),
        ]

    def own_first(row):
        view = row.reshape(2, 2, own)
        view = jnp.where(y_index == 0, view, view[::-1])
        view = jnp.where(core == 0, view, view[:, ::-1])
        return view.transpose(1, 0, 2).reshape(-1)

    positions = own_first(jnp.arange(seq_len, dtype=jnp.int32))
    seg_pair = jnp.stack(
        [own_first(segment_ids[0]), own_first(shift(segment_ids, dx=1)[0])], axis=0
    )
    half_size = HEAD // 2
    frequency = 10000.0 ** (-jnp.arange(half_size, dtype=FULL) * 2.0 / HEAD)
    angles = positions.astype(FULL)[:, None] * frequency[None, :]
    cosine, sine = jnp.cos(angles), jnp.sin(angles)
    turns = 8
    cosine = jnp.concatenate([cosine] * turns + [jnp.ones((seq_len, LANES), FULL)], axis=1)
    sine = jnp.concatenate([-sine, sine] * (turns // 2) + [jnp.zeros((seq_len, LANES), FULL)], axis=1)

    expert_ids = jnp.arange(32, dtype=jnp.int32)
    chosen = jnp.any(routes[:, :, None] == expert_ids[None, None, :], axis=1)
    token_ids = jnp.arange(group, dtype=jnp.int32)
    rank = jnp.sum(
        jnp.where(slot_order[0][:, None] == token_ids[None, :], token_ids[:, None], 0), axis=0
    )
    own_rank = lax.dynamic_slice_in_dim(rank, core * own, own)
    own_chosen = lax.dynamic_slice_in_dim(chosen, core * own, own, 0)
    ahead = (rank[None, :] < own_rank[:, None]).astype(LOW)
    slot = dot(ahead, chosen.astype(LOW), PLAIN)
    kept = (own_chosen & (slot < capacity)).astype(FULL)
    own_chosen = own_chosen.astype(FULL)

    gate_far, up_far, down_far = swap_core(w_gate), swap_core(w_up), swap_core(w_down)
    gate_w, up_w, down_w = (
        (own_half[0], far_half[0])
        for own_half, far_half in ((w_gate, gate_far), (w_up, up_far), (w_down, down_far))
    )

    tokens = 2 * seq_len
    normed, scale_one, qkv, attended, probs, tail = kernel_call(
        attend_body,
        [
            ((tokens, width), LOW),
            ((tokens, 1), FULL),
            ((tokens, a_cols), LOW),
            ((tokens, q_cols), LOW),
            ((6, seq_len, seq_len), FULL),
            ((32, width), FULL),
        ],
        place,
        near_in,
        far_in,
        *a_line,
        cosine,
        sine,
        positions[:, None],
        positions[None, :],
        seg_pair.reshape(-1, 1),
        seg_pair,
    )
    near, far = kernel_call(
        branch_body,
        [((seq_len, width), FULL), ((seq_len, width), LOW)],
        place,
        attended,
        *b_line,
    )
    branch = reduce_tokens(near, far)
    hidden, mixed_ext, gates, scale_two = kernel_call(
        router_body,
        [
            ((own, width), FULL),
            ((own, width + LANES), LOW),
            ((own, 32), FULL),
            ((own, 1), FULL),
        ],
        place,
        layer_input,
        *branch,
        tail,
        own_chosen,
        kept,
    )

    grad_chunks = spread(cotangent)
    hidden_units = 2 * w_gate.shape[1]
    batch = 8 * own
    plain0, plain1, dy0, dy1 = kernel_call(
        upstream_body,
        [((batch, hidden_units), FULL)] * 2 + [((batch, width), LOW)] * 2,
        place,
        *grad_chunks,
        *down_w,
    )
    chunks, inners, d_gates, d_ups, backs = [], [], [], [], []
    for start, plain in ((0, plain0), (own // 2, plain1)):
        chunk = spread(mixed_ext[start : start + own // 2])
        result = kernel_call(
            expert_body,
            [((batch // 4, width + LANES), LOW)] * 4 + [((batch, hidden_units), LOW)] * 3,
            place,
            *chunk,
            plain,
            *gate_w,
            *up_w,
        )
        chunks += chunk
        backs.append(collect(result[:4]))
        inners.append(result[4])
        d_gates.append(result[5])
        d_ups.append(result[6])
    d_hidden, d_branch, d_tail = kernel_call(
        middle_body,
        [((own, width), FULL), ((own, width), LOW), ((32, width), FULL)],
        place,
        *backs[0],
        *backs[1],
        tail,
        gates,
        kept,
        hidden,
        mixed_ext,
        scale_two,
        cotangent,
    )
    out_chunks = kernel_call(
        output_body, [((batch // 2, width), LOW)] * 4, place, *inners, *down_w
    )
    out_parts = collect(out_chunks)
    layer_output = hidden
    for block in out_parts:
        layer_output = layer_output + block.astype(FULL)
    layer_output = layer_output.astype(LOW)
    shape = (3, hidden_units // 2, width)
    expert_mine, expert_send = kernel_call(
        weight_body,
        [(shape, FULL), (shape, LOW)],
        place,
        *chunks,
        dy0,
        dy1,
        *inners,
        *d_gates,
        *d_ups,
    )
    expert_grads = expert_mine + swap_core(expert_send).astype(FULL)

    near, far = gather_tokens(d_branch)
    line_rows = 4 * features

    def line_outs(cols):
        return [((line_rows, cols), FULL)] + [((line_rows, cols), LOW)] * 3

    d_raw, *b_grads = kernel_call(
        backward_body,
        [((tokens, a_cols), LOW), *line_outs(q_cols)],
        place,
        near,
        far,
        *b_line,
        attended,
        probs,
        qkv,
        cosine,
        sine,
        scratch=[pltpu.VMEM((tokens, width), LOW), pltpu.VMEM((tokens, a_cols), FULL)],
    )
    near, far, *a_grads = kernel_call(
        project_body,
        [((seq_len, width), FULL), ((seq_len, width), LOW), *line_outs(a_cols)],
        place,
        d_raw,
        normed,
        near_in,
        far_in,
        scale_one,
        *a_line,
        d_tail,
    )

    def reduce_line(grads):
        total = grads[0]
        for step in range(1, LINE):
            total = total + shift(grads[step], dz=step).astype(FULL)
        return total

    d_normed = reduce_tokens(near, far)
    (grad_input,) = kernel_call(
        final_body, [((own, width), FULL)], place, *d_normed, layer_input, tail, d_hidden
    )
    total = jnp.concatenate([reduce_line(a_grads), reduce_line(b_grads)], axis=1)
    total = total.reshape(4, features, -1)
    low_total = total.astype(LOW)

    def rows_for(step):
        return lax.dynamic_index_in_dim(low_total, mine ^ step, 0, keepdims=False)

    own_total = lax.dynamic_index_in_dim(total, mine, 0, keepdims=False)
    parts = [
        own_total,
        shift(rows_for(1), dy=1).astype(FULL),
        shift(rows_for(2), dx=1).astype(FULL),
        shift(rows_for(3), dx=1, dy=1).astype(FULL),
    ]
    small = parts[0] + parts[1] + parts[2] + parts[3]
    small = small[:, q_cols + 2 * k_cols : a_cols]
    small = small.astype(LOW)
    small = small.astype(FULL) + swap_core(small).astype(FULL)
    columns = jnp.stack(unscramble(parts, x_index, y_index), axis=1)

    def output_of(low, high):
        return columns[:, :, low:high].reshape(features, -1)

    return (
        layer_output,
        grad_input,
        small[:, experts],
        small[:, experts + 1],
        output_of(0, q_cols),
        output_of(q_cols, q_cols + k_cols),
        output_of(q_cols + k_cols, q_cols + 2 * k_cols),
        output_of(a_cols, a_cols + q_cols),
        small[:, :experts],
        expert_grads[0][None],
        expert_grads[1][None],
        expert_grads[2][None],
    )


def solution(mesh):
    in_specs = (
        P((SHARD, CONTEXT, TENSOR), None),
        P(SHARD, None),
        P(CHIPS, None),
        P(CHIPS, None),
        P(CHIPS),
        P(CHIPS),
        P(CHIPS, TENSOR),
        P(CHIPS, TENSOR),
        P(CHIPS, TENSOR),
        P(CHIPS, TENSOR),
        P(CHIPS, None),
        P(CHIPS, TENSOR, None),
        P(CHIPS, TENSOR, None),
        P(CHIPS, TENSOR, None),
        P((SHARD, CONTEXT, TENSOR), None),
    )
    out_specs = (
        P((SHARD, CONTEXT, TENSOR), None),
        P((SHARD, CONTEXT, TENSOR), None),
        P(CHIPS),
        P(CHIPS),
        P(CHIPS, TENSOR),
        P(CHIPS, TENSOR),
        P(CHIPS, TENSOR),
        P(CHIPS, TENSOR),
        P(CHIPS, None),
        P(CHIPS, TENSOR, None),
        P(CHIPS, TENSOR, None),
        P(CHIPS, TENSOR, None),
    )
    sizes = dict(mesh.shape)
    fits = (sizes[SHARD], sizes[CONTEXT], sizes[TENSOR]) == (LINE * PAIR, 2, 2)
    return jax.shard_map(
        fast_block if fits else general_block, mesh=mesh, in_specs=in_specs, out_specs=out_specs, check_vma=False
    )
```

```python
import jax
import jax.numpy as jnp
from jax import lax
from jax.experimental import pallas as pl
from jax.experimental.pallas import tpu as pltpu
from jax.sharding import PartitionSpec as P

SHARD, CONTEXT, TENSOR = "shard", "context", "tensor"
CHIPS = (SHARD, CONTEXT)

HEAD = 64


EPSILON = 1e-05
MASKED = -1e30


def rotary(values, positions, rotation):
    half_size = values.shape[-1] // 2
    frequency = 10000.0 ** (-jnp.arange(half_size, dtype=jnp.float32) * 2.0 / values.shape[-1])
    angles = positions.astype(jnp.float32)[:, None] * frequency[None, :]
    cosine = jnp.cos(angles)[:, None, :]
    sine_part = rotation * jnp.sin(angles)[:, None, :]
    first_half = values[..., :half_size]
    second_half = values[..., half_size:]
    return jnp.concatenate(
        [
            first_half * cosine - second_half * sine_part,
            second_half * cosine + first_half * sine_part,
        ],
        axis=-1,
    )


def slot_numbers(route_rows, priority, expert_count):
    ordered = route_rows[priority]
    flat_routes = ordered.reshape(-1)
    onehot_table = (
        flat_routes[:, None] == jnp.arange(expert_count, dtype=jnp.int32)[None, :]
    ).astype(jnp.int32)
    earlier = jnp.cumsum(onehot_table, axis=0) - onehot_table
    ranked = jnp.sum(earlier * onehot_table, axis=1).reshape(ordered.shape)
    return jnp.zeros(ordered.shape, jnp.int32).at[priority].set(ranked)


def slot_tables(route_rows, priority, capacity, expert_count):
    pair_count = route_rows.shape[0] * route_rows.shape[1]
    slot_index = slot_numbers(route_rows, priority, expert_count)
    kept_mask = slot_index < capacity
    target = jnp.where(kept_mask, route_rows * capacity + slot_index, expert_count * capacity)
    owner_pair = jnp.full((expert_count * capacity + 1,), pair_count, jnp.int32)
    owner_pair = owner_pair.at[target.reshape(-1)].set(jnp.arange(pair_count, dtype=jnp.int32))[:-1]
    return (target, owner_pair)


def general_block(
    layer_input,
    segment_ids,
    routes,
    slot_order,
    norm1_gain,
    norm2_gain,
    w_query,
    w_key,
    w_value,
    w_out,
    w_router,
    w_gate,
    w_up,
    w_down,
    cotangent,
):
    n_tensor = lax.axis_size(TENSOR)
    tensor_index = lax.axis_index(TENSOR)
    context_index = lax.axis_index(CONTEXT)
    own_rows = layer_input.shape[0]
    tok_rows = own_rows * n_tensor
    full_width = layer_input.shape[1]
    choose_count = routes.shape[1]
    expert_count = w_router.shape[1]
    pair_count = tok_rows * choose_count
    capacity = 5 * tok_rows * choose_count // (4 * expert_count)
    cap_part = capacity // n_tensor
    slot_start = tensor_index * cap_part
    head_size = HEAD
    query_heads = w_query.shape[1] // head_size
    key_heads = w_key.shape[1] // head_size
    group_size = query_heads // key_heads
    seq_len = segment_ids.shape[1]
    block_size = min(256, seq_len)
    block_count = seq_len // block_size
    row_start = tensor_index * own_rows
    input_full, grad_full, gate_whole, up_whole, down_whole = (
        lax.all_gather(layer_input, TENSOR, axis=0, tiled=True),
        lax.all_gather(cotangent, TENSOR, axis=0, tiled=True),
        lax.all_gather(w_gate, TENSOR, axis=1, tiled=True),
        lax.all_gather(w_up, TENSOR, axis=1, tiled=True),
        lax.all_gather(w_down, TENSOR, axis=1, tiled=True),
    )
    gain_one, gain_two, query_w, key_w, value_w, out_w, router_w = (
        lax.all_gather(norm1_gain, CHIPS, axis=0, tiled=True),
        lax.all_gather(norm2_gain, CHIPS, axis=0, tiled=True),
        lax.all_gather(w_query, CHIPS, axis=0, tiled=True),
        lax.all_gather(w_key, CHIPS, axis=0, tiled=True),
        lax.all_gather(w_value, CHIPS, axis=0, tiled=True),
        lax.all_gather(w_out, CHIPS, axis=0, tiled=True),
        lax.all_gather(w_router, CHIPS, axis=0, tiled=True),
    )
    gain_one = gain_one.astype(jnp.float32)
    gain_two = gain_two.astype(jnp.float32)
    inputs = input_full.astype(jnp.float32)
    scale_one = lax.rsqrt(jnp.mean(inputs * inputs, axis=1, keepdims=True) + EPSILON)
    normed = (inputs * scale_one * gain_one).astype(jnp.bfloat16)
    query_raw = jnp.dot(normed, query_w, preferred_element_type=jnp.float32)
    key_raw = jnp.dot(normed, key_w, preferred_element_type=jnp.float32)
    value_low = jnp.dot(normed, value_w, preferred_element_type=jnp.float32).astype(jnp.bfloat16)
    positions = context_index * tok_rows + jnp.arange(tok_rows, dtype=jnp.int32)
    queries = rotary(query_raw.reshape(tok_rows, query_heads, head_size), positions, 1.0).astype(
        jnp.bfloat16
    )
    queries = queries.reshape(tok_rows, key_heads, group_size, head_size)
    keys_low = rotary(key_raw.reshape(tok_rows, key_heads, head_size), positions, 1.0).astype(
        jnp.bfloat16
    )
    keys_low = keys_low.reshape(tok_rows, key_heads * head_size)
    keys_all, values_all = (
        lax.all_gather(keys_low, CONTEXT, axis=0, tiled=True),
        lax.all_gather(value_low, CONTEXT, axis=0, tiled=True),
    )
    seg_row = segment_ids[0]
    seg_query = lax.dynamic_slice_in_dim(seg_row, context_index * tok_rows, tok_rows)
    key_blocks = keys_all.reshape(block_count, block_size, key_heads, head_size)
    value_blocks = values_all.reshape(block_count, block_size, key_heads, head_size)
    seg_blocks = seg_row.reshape(block_count, block_size)
    block_starts = jnp.arange(block_count, dtype=jnp.int32) * block_size
    block_inputs = (key_blocks, value_blocks, block_starts, seg_blocks)

    def block_scores(key_block, key_start, seg_block):
        raw_scores = (
            jnp.einsum("qhgd,khd->hgqk", queries, key_block, preferred_element_type=jnp.float32)
            * 0.125
        )
        key_pos = key_start + jnp.arange(key_block.shape[0], dtype=jnp.int32)
        allowed = (key_pos[None, :] <= positions[:, None]) & (
            seg_block[None, :] == seg_query[:, None]
        )
        return (raw_scores, allowed[None, None])

    def running_max(running, block_in):
        row_max, row_sum = running
        key_block, value_block, key_start, seg_block = block_in
        raw_scores, allowed = block_scores(key_block, key_start, seg_block)
        new_max = jnp.maximum(row_max, jnp.max(jnp.where(allowed, raw_scores, MASKED), axis=-1))
        terms = jnp.where(allowed, jnp.exp(raw_scores - new_max[..., None]), 0.0)
        row_sum = row_sum * jnp.exp(row_max - new_max) + jnp.sum(terms, axis=-1)
        return ((new_max, row_sum), None)

    start_max = jnp.full((key_heads, group_size, tok_rows), MASKED, jnp.float32)
    start_sum = jnp.zeros((key_heads, group_size, tok_rows), jnp.float32)
    (row_max, row_sum), unused = lax.scan(running_max, (start_max, start_sum), block_inputs)
    log_total = row_max + jnp.log(row_sum)

    def attend_step(accum, block_in):
        key_block, value_block, key_start, seg_block = block_in
        raw_scores, allowed = block_scores(key_block, key_start, seg_block)
        probs_low = jnp.where(allowed, jnp.exp(raw_scores - log_total[..., None]), 0.0).astype(
            jnp.bfloat16
        )
        accum = accum + jnp.einsum(
            "hgqk,khd->qhgd", probs_low, value_block, preferred_element_type=jnp.float32
        )
        return (accum, None)

    attn_start = jnp.zeros((tok_rows, key_heads, group_size, head_size), jnp.float32)
    attended_f, unused = lax.scan(attend_step, attn_start, block_inputs)
    attended = attended_f.astype(jnp.bfloat16).reshape(tok_rows, query_heads * head_size)
    branch_part = lax.dot_general(
        attended, out_w, (((1,), (1,)), ((), ())), preferred_element_type=jnp.float32
    )
    branch = lax.psum(branch_part.astype(jnp.bfloat16), TENSOR).astype(jnp.float32)
    hidden_state = inputs + branch
    scale_two = lax.rsqrt(jnp.mean(hidden_state * hidden_state, axis=1, keepdims=True) + EPSILON)
    mixed_in = (hidden_state * scale_two * gain_two).astype(jnp.bfloat16)
    logits = jnp.dot(mixed_in, router_w, preferred_element_type=jnp.float32)
    route_onehot = routes[:, :, None] == jnp.arange(expert_count, dtype=jnp.int32)[None, None, :]
    picked = jnp.sum(jnp.where(route_onehot, logits[:, None, :], 0.0), axis=-1)
    gate_probs = jax.nn.softmax(picked, axis=-1)
    target, owner_pair = slot_tables(routes, slot_order[0], capacity, expert_count)
    owner_local = lax.dynamic_slice_in_dim(
        owner_pair.reshape(expert_count, capacity), slot_start, cap_part, 1
    )
    token_local = owner_local // choose_count
    flat_owner = owner_local.reshape(-1)
    flat_token = token_local.reshape(-1)
    mixed_pad = jnp.concatenate([mixed_in, jnp.zeros((1, full_width), jnp.bfloat16)], axis=0)
    send_rows = mixed_pad[token_local]
    rows_in = lax.all_to_all(
        send_rows, CHIPS, split_axis=0, concat_axis=1, tiled=True
    )
    gate_act = jnp.einsum("erd,efd->erf", rows_in, gate_whole, preferred_element_type=jnp.float32)
    up_act = jnp.einsum("erd,efd->erf", rows_in, up_whole, preferred_element_type=jnp.float32)
    inner_low = (jax.nn.silu(gate_act) * up_act).astype(jnp.bfloat16)
    expert_low = jnp.einsum(
        "erf,efd->erd", inner_low, down_whole, preferred_element_type=jnp.float32
    ).astype(jnp.bfloat16)
    returned = lax.all_to_all(
        expert_low, CHIPS, split_axis=1, concat_axis=0, tiled=True
    )
    gate_pad = jnp.concatenate([gate_probs.reshape(-1), jnp.zeros((1,), jnp.float32)], axis=0)
    gate_local = gate_pad[owner_local]
    grad_pad = jnp.concatenate([grad_full, jnp.zeros((1, full_width), jnp.bfloat16)], axis=0)
    dy_rows = grad_pad[token_local].astype(jnp.float32)
    returned_f = returned.astype(jnp.float32)
    dgate_slot = jnp.sum(returned_f * dy_rows, axis=2)
    dgate_part = (
        jnp.zeros((pair_count + 1,), jnp.float32)
        .at[flat_owner]
        .add(dgate_slot.reshape(-1))[:pair_count]
    )
    dgate_part = dgate_part.reshape(tok_rows, choose_count)
    all_slots = lax.all_gather(returned, TENSOR, axis=1, tiled=True)
    slots_pad = jnp.concatenate(
        [
            all_slots.reshape(expert_count * capacity, full_width),
            jnp.zeros((1, full_width), jnp.bfloat16),
        ],
        axis=0,
    )
    own_target = lax.dynamic_slice_in_dim(target, row_start, own_rows, 0)
    own_gate = lax.dynamic_slice_in_dim(gate_probs, row_start, own_rows, 0)
    own_picked = (
        slots_pad[own_target.reshape(-1)]
        .reshape(own_rows, choose_count, full_width)
        .astype(jnp.float32)
    )
    mixture_own = jnp.sum(own_picked * own_gate[:, :, None], axis=1)
    hidden_own = lax.dynamic_slice_in_dim(hidden_state, row_start, own_rows, 0)
    layer_output = (hidden_own + mixture_own).astype(jnp.bfloat16)
    grad_outer = grad_full.astype(jnp.float32)
    grad_send = (dy_rows * gate_local[:, :, None]).astype(jnp.bfloat16)
    grad_rows = lax.all_to_all(
        grad_send, CHIPS, split_axis=0, concat_axis=1, tiled=True
    )
    grad_inner = jnp.einsum(
        "erd,efd->erf", grad_rows, down_whole, preferred_element_type=jnp.float32
    )
    down_grad = jnp.einsum("erf,erd->efd", inner_low, grad_rows, preferred_element_type=jnp.float32)
    sigmoid_gate = jax.nn.sigmoid(gate_act)
    grad_gate_act = (
        grad_inner * up_act * sigmoid_gate * (1.0 + gate_act * (1.0 - sigmoid_gate))
    ).astype(jnp.bfloat16)
    grad_up_act = (grad_inner * gate_act * sigmoid_gate).astype(jnp.bfloat16)
    gate_grad = jnp.einsum(
        "erf,erd->efd", grad_gate_act, rows_in, preferred_element_type=jnp.float32
    )
    up_grad = jnp.einsum("erf,erd->efd", grad_up_act, rows_in, preferred_element_type=jnp.float32)
    rows_back = jnp.einsum(
        "erf,efd->erd", grad_gate_act, gate_whole, preferred_element_type=jnp.float32
    )
    rows_back = rows_back + jnp.einsum(
        "erf,efd->erd", grad_up_act, up_whole, preferred_element_type=jnp.float32
    )
    back_rows = lax.all_to_all(
        rows_back.astype(jnp.bfloat16),
        CHIPS,
        split_axis=1,
        concat_axis=0,
        tiled=True,
    )
    dmixed_part = (
        jnp.zeros((tok_rows + 1, full_width), jnp.float32)
        .at[flat_token]
        .add(back_rows.astype(jnp.float32).reshape(-1, full_width))[:tok_rows]
    )
    dmixed_experts, dgate = (
        lax.psum(dmixed_part.astype(jnp.bfloat16), TENSOR).astype(jnp.float32),
        lax.psum(dgate_part.astype(jnp.bfloat16), TENSOR).astype(jnp.float32),
    )
    dpicked = gate_probs * (dgate - jnp.sum(gate_probs * dgate, axis=1, keepdims=True))
    dlogits = jnp.sum(jnp.where(route_onehot, dpicked[:, :, None], 0.0), axis=1).astype(
        jnp.bfloat16
    )
    drouter = lax.dot_general(
        mixed_in, dlogits, (((0,), (0,)), ((), ())), preferred_element_type=jnp.float32
    )
    dmixed = dmixed_experts + lax.dot_general(
        dlogits, router_w, (((1,), (1,)), ((), ())), preferred_element_type=jnp.float32
    )
    dgain_two = jnp.sum(dmixed * hidden_state * scale_two, axis=0)
    inner_two = jnp.sum(dmixed * gain_two * hidden_state, axis=1, keepdims=True) / full_width
    dhidden = grad_outer + dmixed * gain_two * scale_two - hidden_state * scale_two**3 * inner_two
    dbranch = dhidden.astype(jnp.bfloat16)
    dout_w = lax.dot_general(
        dbranch, attended, (((0,), (0,)), ((), ())), preferred_element_type=jnp.float32
    )
    dattended = jnp.dot(dbranch, out_w, preferred_element_type=jnp.float32).astype(jnp.bfloat16)
    dattended = dattended.reshape(tok_rows, key_heads, group_size, head_size)
    row_delta = jnp.einsum("qhgd,qhgd->hgq", dattended.astype(jnp.float32), attended_f)

    def backward_step(dquery_acc, block_in):
        key_block, value_block, key_start, seg_block = block_in
        raw_scores, allowed = block_scores(key_block, key_start, seg_block)
        attn_probs = jnp.where(allowed, jnp.exp(raw_scores - log_total[..., None]), 0.0)
        probs_low = attn_probs.astype(jnp.bfloat16)
        dprobs = jnp.einsum(
            "qhgd,khd->hgqk", dattended, value_block, preferred_element_type=jnp.float32
        )
        dscores = (attn_probs * (dprobs - row_delta[..., None])).astype(jnp.bfloat16)
        dquery_acc = dquery_acc + jnp.einsum(
            "hgqk,khd->qhgd", dscores, key_block, preferred_element_type=jnp.float32
        )
        dkey_block = (
            jnp.einsum("hgqk,qhgd->khd", dscores, queries, preferred_element_type=jnp.float32)
            * 0.125
        )
        dvalue_block = jnp.einsum(
            "hgqk,qhgd->khd", probs_low, dattended, preferred_element_type=jnp.float32
        )
        return (dquery_acc, (dkey_block, dvalue_block))

    dquery_acc, (dkey_blocks, dvalue_blocks) = lax.scan(backward_step, attn_start, block_inputs)
    dkeys_seq = dkey_blocks.reshape(seq_len, key_heads * head_size)
    dvalues_seq = dvalue_blocks.reshape(seq_len, key_heads * head_size)
    dkeys, dvalues = (
        lax.psum_scatter(
            dkeys_seq.astype(jnp.bfloat16), CONTEXT, scatter_dimension=0, tiled=True
        ).astype(jnp.float32),
        lax.psum_scatter(
            dvalues_seq.astype(jnp.bfloat16), CONTEXT, scatter_dimension=0, tiled=True
        ).astype(jnp.float32),
    )
    dquery_raw = rotary(
        (dquery_acc * 0.125).reshape(tok_rows, query_heads, head_size), positions, -1.0
    )
    dquery_raw = dquery_raw.astype(jnp.bfloat16).reshape(tok_rows, query_heads * head_size)
    dkey_raw = rotary(dkeys.reshape(tok_rows, key_heads, head_size), positions, -1.0)
    dkey_raw = dkey_raw.astype(jnp.bfloat16).reshape(tok_rows, key_heads * head_size)
    dvalue_low = dvalues.astype(jnp.bfloat16)
    contract_rows = (((0,), (0,)), ((), ()))
    contract_cols = (((1,), (1,)), ((), ()))
    dquery_w = lax.dot_general(
        normed, dquery_raw, contract_rows, preferred_element_type=jnp.float32
    )
    dkey_w = lax.dot_general(normed, dkey_raw, contract_rows, preferred_element_type=jnp.float32)
    dvalue_w = lax.dot_general(
        normed, dvalue_low, contract_rows, preferred_element_type=jnp.float32
    )
    dnormed_part = lax.dot_general(
        dquery_raw, query_w, contract_cols, preferred_element_type=jnp.float32
    )
    dnormed_part = dnormed_part + lax.dot_general(
        dkey_raw, key_w, contract_cols, preferred_element_type=jnp.float32
    )
    dnormed_part = dnormed_part + lax.dot_general(
        dvalue_low, value_w, contract_cols, preferred_element_type=jnp.float32
    )
    dnormed = lax.psum(dnormed_part.astype(jnp.bfloat16), TENSOR).astype(jnp.float32)
    dgain_one = jnp.sum(dnormed * inputs * scale_one, axis=0)
    inner_one = jnp.sum(dnormed * gain_one * inputs, axis=1, keepdims=True) / full_width
    dinput = dhidden + dnormed * gain_one * scale_one - inputs * scale_one**3 * inner_one
    grad_input = lax.dynamic_slice_in_dim(dinput, row_start, own_rows, 0)
    grad_gate, grad_up, grad_down = (
        lax.psum_scatter(
            gate_grad.astype(jnp.bfloat16), TENSOR, scatter_dimension=1, tiled=True
        ).astype(jnp.float32),
        lax.psum_scatter(
            up_grad.astype(jnp.bfloat16), TENSOR, scatter_dimension=1, tiled=True
        ).astype(jnp.float32),
        lax.psum_scatter(
            down_grad.astype(jnp.bfloat16), TENSOR, scatter_dimension=1, tiled=True
        ).astype(jnp.float32),
    )
    grad_norm1, grad_norm2, grad_query, grad_key, grad_value, grad_out, grad_router = (
        lax.psum_scatter(
            dgain_one.astype(jnp.bfloat16), CHIPS, scatter_dimension=0, tiled=True
        ).astype(jnp.float32),
        lax.psum_scatter(
            dgain_two.astype(jnp.bfloat16), CHIPS, scatter_dimension=0, tiled=True
        ).astype(jnp.float32),
        lax.psum_scatter(
            dquery_w.astype(jnp.bfloat16), CHIPS, scatter_dimension=0, tiled=True
        ).astype(jnp.float32),
        lax.psum_scatter(
            dkey_w.astype(jnp.bfloat16), CHIPS, scatter_dimension=0, tiled=True
        ).astype(jnp.float32),
        lax.psum_scatter(
            dvalue_w.astype(jnp.bfloat16), CHIPS, scatter_dimension=0, tiled=True
        ).astype(jnp.float32),
        lax.psum_scatter(
            dout_w.astype(jnp.bfloat16), CHIPS, scatter_dimension=0, tiled=True
        ).astype(jnp.float32),
        lax.psum_scatter(
            drouter.astype(jnp.bfloat16), CHIPS, scatter_dimension=0, tiled=True
        ).astype(jnp.float32),
    )
    return (
        layer_output,
        grad_input,
        grad_norm1,
        grad_norm2,
        grad_query,
        grad_key,
        grad_value,
        grad_out,
        grad_router,
        grad_gate,
        grad_up,
        grad_down,
    )


LINE, PAIR = 4, 2
LANES = 128
ROWS = ((0,), (0,))
COLS = ((1,), (1,))
PLAIN = ((1,), (0,))
LOW, FULL = jnp.bfloat16, jnp.float32


def shift(block, dz=0, dx=0, dy=0):
    pairs = []
    for z in range(LINE):
        for x in range(PAIR):
            for y in range(PAIR):
                target = (((z ^ dz) * PAIR + (x ^ dx)) * PAIR) + (y ^ dy)
                pairs.append(((z * PAIR + x) * PAIR + y, target))
    return lax.ppermute(block, CHIPS, pairs)


def swap_core(block):
    return lax.ppermute(block, TENSOR, [(0, 1), (1, 0)])


def plane(block):
    return [shift(block, dy=1), shift(block, dx=1), shift(block, dx=1, dy=1)]


def dot(left, right, dims):
    return lax.dot_general(left, right, (dims, ((), ())), preferred_element_type=FULL)


def kernel_call(body, outs, *operands, scratch=()):
    specs = [pl.BlockSpec(memory_space=pltpu.SMEM)]
    specs += [pl.BlockSpec(memory_space=pltpu.VMEM) for _ in operands[1:]]
    return pl.pallas_call(
        body,
        out_shape=[jax.ShapeDtypeStruct(shape, kind) for shape, kind in outs],
        in_specs=specs,
        out_specs=[pl.BlockSpec(memory_space=pltpu.VMEM) for _ in outs],
        scratch_shapes=list(scratch),
        compiler_params=pltpu.CompilerParams(vmem_limit_bytes=56 * 1024 * 1024),
    )(*operands)


def line_slice(place, step, size):
    return pl.ds(pl.multiple_of((place[0] ^ step) * size, LANES), size)


def half_turn(values):
    width = values.shape[1]
    lane = lax.broadcasted_iota(jnp.int32, values.shape, 1)
    up = pltpu.roll(values, width - HEAD // 2, 1)
    down = pltpu.roll(values, HEAD // 2, 1)
    return jnp.where(lane % HEAD < HEAD // 2, up, down)


def twice(table):
    return jnp.concatenate([table, table], axis=0)


def join_tokens(near, far):
    count = near.shape[0] // 2
    return jnp.concatenate([near[:count], far[:count], near[count:], far[count:]], axis=0)


def split_tokens(values):
    count = values.shape[0] // 4
    near = jnp.concatenate([values[:count], values[2 * count : 3 * count]], axis=0)
    far = jnp.concatenate([values[count : 2 * count], values[3 * count :]], axis=0)
    return near, far


def pack_body(place, query, key, value, extra, out_w, s0, s1, s2, s3, packs):
    q_cols, k_cols = query.shape[1] // 4, key.shape[1] // 4
    for part in range(4):
        q_span = slice(part * q_cols, (part + 1) * q_cols)
        k_span = slice(part * k_cols, (part + 1) * k_cols)
        packs[part] = jnp.concatenate(
            [query[:, q_span], key[:, k_span], value[:, k_span], extra[...], out_w[:, q_span]],
            axis=1,
        )
    for step, out in enumerate((s0, s1, s2, s3)):
        out[...] = packs[place[2] ^ step]


def rows_body(place, p0, p1, p2, p3, a_out, b_out, rest):
    count, a_cols = p0.shape[0], a_out.shape[1]
    for step, part in enumerate((p0, p1, p2, p3)):
        span = pl.ds(pl.multiple_of((place[2] ^ step) * count, 16), count)
        a_out[span, :] = part[:, :a_cols]
        rest[span, : part.shape[1] - a_cols] = part[:, a_cols:].astype(FULL)
    b_out[...] = rest[...].T[: b_out.shape[0]].astype(LOW)


def total_body(place, mine, r1, r2, r3, own_out, s1, s2, s3, total):
    size = mine.shape[1]
    value = mine[...] + r1[...].astype(FULL) + r2[...].astype(FULL) + r3[...].astype(FULL)
    total[:, :size] = value[:size]
    pad = jnp.zeros((total.shape[1] - mine.shape[0], size), FULL)
    total[:, size:] = jnp.concatenate([value[size:], pad], axis=0).T
    count, cols = own_out.shape
    for step, out in enumerate((own_out, s1, s2, s3)):
        span = pl.ds(pl.multiple_of((place[2] ^ step) * count, 16), count)
        out[...] = total[span, :cols].astype(out.dtype)


def gradient_body(
    place, own, r1, r2, r3, query_out, key_out, value_out, out_out, small_out, parts
):
    small = 0.0
    q_cols, k_cols = query_out.shape[1] // 4, key_out.shape[1] // 4
    ends = (q_cols, q_cols + k_cols, q_cols + 2 * k_cols, q_cols + 2 * k_cols + HEAD)
    for step, part in enumerate((own, r1, r2, r3)):
        value = part[...].astype(FULL)
        parts[place[2] ^ step] = value
        small = small + value[:, ends[2] : ends[3]]
    small_out[...] = small.astype(LOW)
    pieces = [parts[n] for n in range(4)]
    query_out[...] = jnp.concatenate([piece[:, : ends[0]] for piece in pieces], axis=1)
    key_out[...] = jnp.concatenate([piece[:, ends[0] : ends[1]] for piece in pieces], axis=1)
    value_out[...] = jnp.concatenate([piece[:, ends[1] : ends[2]] for piece in pieces], axis=1)
    out_out[...] = jnp.concatenate([piece[:, ends[3] :] for piece in pieces], axis=1)


def attend_body(
    place, near, far, w0, w1, w2, w3, cosine, sine, pos_col, pos_row, seg_col, seg_row,
    normed_out, scale_out, qkv_out, attended_out, probs_out, tail_out,
):
    weights = (w0, w1, w2, w3)
    size = w0.shape[0]
    for step, weight in enumerate(weights):
        turned = weight[:, 2 * LANES :].astype(FULL).T
        tail_out[:, line_slice(place, step, size)] = turned[HEAD : HEAD + 32]
    inputs = join_tokens(near[...], far[...]).astype(FULL)
    scale = lax.rsqrt(jnp.mean(inputs * inputs, axis=1, keepdims=True) + EPSILON)
    scale_out[...] = scale
    normed_out[...] = (inputs * scale * tail_out[16:17, :]).astype(LOW)
    raw = 0.0
    for step, weight in enumerate(weights):
        raw = raw + dot(normed_out[:, line_slice(place, step, size)], weight[...], PLAIN)
    turned = raw * twice(cosine[...]) + half_turn(raw) * twice(sine[...])
    qkv_out[...] = turned.astype(LOW)
    length = raw.shape[0] // 2
    for seq in range(2):
        span = slice(seq * length, (seq + 1) * length)
        allowed = (pos_row[...] <= pos_col[...]) & (seg_row[seq : seq + 1] == seg_col[span])
        keys = qkv_out[span, 3 * HEAD : 4 * HEAD]
        values = qkv_out[span, 4 * HEAD : 5 * HEAD]
        heads = []
        for head in range(3):
            queries = qkv_out[span, head * HEAD : (head + 1) * HEAD]
            scores = jnp.where(allowed, dot(queries, keys, COLS) * 0.125, MASKED)
            top = jnp.max(scores, axis=1, keepdims=True)
            terms = jnp.where(allowed, jnp.exp(scores - top), 0.0)
            probs = terms / jnp.sum(terms, axis=1, keepdims=True)
            probs_out[seq * 3 + head] = probs
            heads.append(dot(probs.astype(LOW), values, PLAIN))
        attended_out[span] = jnp.concatenate(heads, axis=1).astype(LOW)


def branch_body(place, attended, o0, o1, o2, o3, near_out, far_out):
    for step, weight in enumerate((o0, o1, o2, o3)):
        near, far = split_tokens(dot(attended[...], weight[...], PLAIN))
        span = line_slice(place, step, weight.shape[1])
        near_out[:, span] = near
        far_out[:, span] = far.astype(LOW)


def two_parts(value):
    high = value.astype(LOW)
    return high, (value - high.astype(FULL)).astype(LOW)


def router_body(
    place, inputs, mine, r1, r2, r3, tail, chosen, kept,
    hidden_out, mixed_out, gates_out, scale_out,
):
    hidden = inputs[...].astype(FULL) + mine[...].astype(FULL)
    hidden = hidden + r1[...].astype(FULL) + r2[...].astype(FULL) + r3[...].astype(FULL)
    hidden_out[...] = hidden
    scale = lax.rsqrt(jnp.mean(hidden * hidden, axis=1, keepdims=True) + EPSILON)
    scale_out[...] = scale
    mixed = (hidden * scale * tail[17:18, :]).astype(LOW)
    width = mixed.shape[1]
    mixed_out[:, :width] = mixed
    logits = dot(mixed, tail[...].astype(LOW), COLS)
    on = chosen[...] > 0.0
    best = jnp.max(jnp.where(on, logits, MASKED), axis=1, keepdims=True)
    gates = jnp.where(on, jnp.exp(logits - best), 0.0)
    gates = gates / jnp.sum(gates, axis=1, keepdims=True)
    gates_out[...] = gates
    high, rest = two_parts(gates * kept[...])
    blank = jnp.zeros((mixed.shape[0], LANES - 64), LOW)
    mixed_out[:, width:] = jnp.concatenate([high, rest, blank], axis=1)


def upstream_body(place, chunk_a, chunk_b, own_w, far_w, plain0, plain1, dy0, dy1):
    for at, ref in enumerate((chunk_a, chunk_b)):
        value = ref[...]
        flat = jnp.concatenate([dot(value, own_w[...], COLS), dot(value, far_w[...], COLS)], axis=1)
        for block in range(4):
            for batch, (plain, copy) in enumerate(((plain0, dy0), (plain1, dy1))):
                source = slice(block * 64 + batch * 32, block * 64 + batch * 32 + 32)
                target = slice(at * 128 + block * 32, at * 128 + block * 32 + 32)
                plain[target] = flat[source]
                copy[target] = value[source]


def expert_body(
    place, chunk_a, chunk_b, plain, gate_own, gate_far, up_own, up_far,
    back_a, back_b, inner_out, d_gate_out, d_up_out,
):
    part, width = gate_own.shape
    rows = jnp.concatenate([chunk_a[:, :width], chunk_b[:, :width]], axis=0)
    tails = jnp.concatenate([chunk_a[:, width:], chunk_b[:, width:]], axis=0).astype(FULL)
    lane = lax.broadcasted_iota(jnp.int32, tails.shape, 1)
    is_top, is_rest = lane == place[1], lane == place[1] + 32
    gate = jnp.sum(jnp.where(is_top | is_rest, tails, 0.0), axis=1, keepdims=True)
    d_gate = 0.0
    d_rows = 0.0
    for half, (gate_w, up_w) in enumerate(((gate_own, up_own), (gate_far, up_far))):
        cols = slice(half * part, (half + 1) * part)
        gate_act = dot(rows, gate_w[...], COLS)
        up_act = dot(rows, up_w[...], COLS)
        sig = 1.0 / (1.0 + jnp.exp(-gate_act))
        silu = gate_act * sig
        inner = silu * up_act
        d_plain = plain[:, cols]
        d_gate = d_gate + jnp.sum(inner * d_plain, axis=1, keepdims=True)
        inner_out[:, cols] = (inner * gate).astype(LOW)
        d_inner = d_plain * gate
        d_gate_act = (d_inner * up_act * sig * (1.0 + gate_act * (1.0 - sig))).astype(LOW)
        d_up_act = (d_inner * silu).astype(LOW)
        d_gate_out[:, cols] = d_gate_act
        d_up_out[:, cols] = d_up_act
        d_rows = d_rows + dot(d_gate_act, gate_w[...], PLAIN)
        d_rows = d_rows + dot(d_up_act, up_w[...], PLAIN)
    high, rest = two_parts(d_gate)
    zero = jnp.zeros((), FULL)
    tail = jnp.where(is_top, high.astype(FULL), jnp.where(is_rest, rest.astype(FULL), zero))
    count = back_a.shape[0]
    for at, back in enumerate((back_a, back_b)):
        span = slice(at * count, (at + 1) * count)
        back[:, :width] = d_rows[span].astype(LOW)
        back[:, width:] = tail[span].astype(LOW)


def output_body(place, inner0, inner1, own_w, far_w, out_a, out_b):
    part = own_w.shape[0]
    for batch, inner in enumerate((inner0, inner1)):
        for at, out in enumerate((out_a, out_b)):
            value = inner[at * 128 : at * 128 + 128]
            rows = dot(value[:, :part], own_w[...], PLAIN) + dot(value[:, part:], far_w[...], PLAIN)
            for block in range(4):
                target = slice(block * 64 + batch * 32, block * 64 + batch * 32 + 32)
                out[target] = rows[block * 32 : block * 32 + 32].astype(LOW)


def weight_body(place, *refs):
    mine_out, send_out = refs[24:]
    part, width = mine_out.shape[1:]
    rows = [
        jnp.concatenate([refs[2 * n][:, :width], refs[2 * n + 1][:, :width]], axis=0)
        for n in range(4)
    ]
    dy = [ref[...] for ref in refs[8:12]]
    inner, d_gate, d_up = refs[12:16], refs[16:20], refs[20:24]
    for which, (lefts, rights) in enumerate(((d_gate, rows), (d_up, rows), (inner, dy))):
        for half in range(2):
            cols = slice(half * part, (half + 1) * part)
            total = 0.0
            for left, right in zip(lefts, rights):
                total = total + dot(left[:, cols], right, ROWS)
            if half == 0:
                mine_out[which] = total
            else:
                send_out[which] = total.astype(LOW)


def middle_body(
    place, a0, a1, a2, a3, b0, b1, b2, b3, tail, gates, kept, hidden_in, mixed, scale_in, grad,
    d_hidden_out, d_branch_out, d_tail_out,
):
    def total(refs):
        value = refs[0][...].astype(FULL)
        for ref in refs[1:]:
            value = value + ref[...].astype(FULL)
        return value

    back = jnp.concatenate([total((a0, a1, a2, a3)), total((b0, b1, b2, b3))], axis=0)
    width = grad.shape[1]
    d_gates = (back[:, width : width + 32] + back[:, width + 32 : width + 64]) * kept[...]
    gate = gates[...]
    d_logits = gate * (d_gates - jnp.sum(gate * d_gates, axis=1, keepdims=True))
    d_logits = d_logits.astype(LOW)
    d_router = dot(d_logits, mixed[:, :width], ROWS)
    d_mixed = back[:, :width] + dot(d_logits, tail[...].astype(LOW), PLAIN)
    hidden, scale, gain = hidden_in[...], scale_in[...], tail[17:18, :]
    d_gain = jnp.sum(d_mixed * hidden * scale, axis=0, keepdims=True)
    row = lax.broadcasted_iota(jnp.int32, d_router.shape, 0)
    d_tail_out[...] = jnp.where(row == 17, d_gain, d_router)
    scaled = d_mixed * gain
    inner = jnp.sum(scaled * hidden, axis=1, keepdims=True) / width
    d_hidden = grad[...].astype(FULL) + scaled * scale - hidden * (scale * scale * scale) * inner
    d_hidden_out[...] = d_hidden
    d_branch_out[...] = d_hidden.astype(LOW)


def backward_body(
    place, near, far, o0, o1, o2, o3, probs_in, qkv, cosine, sine,
    d_raw_out, d_branch, d_turned,
):
    d_branch[...] = join_tokens(near[...], far[...])
    size = o0.shape[1]
    d_attended = 0.0
    for step, weight in enumerate((o0, o1, o2, o3)):
        piece = d_branch[:, line_slice(place, step, size)]
        d_attended = d_attended + dot(piece, weight[...], COLS)
    d_attended = d_attended.astype(LOW)
    length = d_attended.shape[0] // 2
    for seq in range(2):
        span = slice(seq * length, (seq + 1) * length)
        keys = qkv[span, 3 * HEAD : 4 * HEAD]
        values = qkv[span, 4 * HEAD : 5 * HEAD]
        pieces, d_keys, d_values = [], 0.0, 0.0
        for head in range(3):
            queries = qkv[span, head * HEAD : (head + 1) * HEAD]
            d_head = d_attended[span, head * HEAD : (head + 1) * HEAD]
            probs = probs_in[seq * 3 + head]
            d_probs = dot(d_head, values, COLS)
            delta = jnp.sum(probs * d_probs, axis=1, keepdims=True)
            d_scores = (probs * (d_probs - delta)).astype(LOW)
            pieces.append(dot(d_scores, keys, PLAIN) * 0.125)
            d_keys = d_keys + dot(d_scores, queries, ROWS) * 0.125
            d_values = d_values + dot(probs.astype(LOW), d_head, ROWS)
        blank = jnp.zeros((length, HEAD), FULL)
        d_turned[span] = jnp.concatenate([*pieces, d_keys, d_values, blank], axis=1)
    value = d_turned[...]
    turned = value * twice(cosine[...]) - half_turn(value) * twice(sine[...])
    d_raw_out[...] = turned.astype(LOW)


def project_body(
    place, d_raw, normed, near, far, scale, w0, w1, w2, w3, d_tail, d_branch, attended,
    near_out, far_out, e0, e1, e2, e3,
):
    size = w0.shape[0]
    d_value = d_raw[...]
    for step, (weight, out) in enumerate(((w0, e0), (w1, e1), (w2, e2), (w3, e3))):
        span = line_slice(place, step, size)
        d_normed = dot(d_value, weight[...], COLS)
        inputs = join_tokens(near[:, span], far[:, span]).astype(FULL)
        d_gain = jnp.sum(d_normed * inputs * scale[...], axis=0, keepdims=True)
        d_near, d_far = split_tokens(d_normed)
        near_out[:, span] = d_near
        far_out[:, span] = d_far.astype(LOW)
        tail = d_tail[:, span]
        row = lax.broadcasted_iota(jnp.int32, tail.shape, 0)
        tail = jnp.where(row == 16, d_gain, tail)
        pad = jnp.zeros((HEAD, size), FULL)
        tail = jnp.concatenate([pad, tail, pad[:32]], axis=0).T
        d_weight = dot(normed[:, span], d_value, ROWS)
        out[:size, : 2 * LANES] = d_weight[:, : 2 * LANES].astype(out.dtype)
        out[:size, 2 * LANES :] = (d_weight[:, 2 * LANES :] + tail).astype(out.dtype)
        out[size:] = dot(attended[...], d_branch[:, span], ROWS).astype(out.dtype)


def final_body(place, mine, r1, r2, r3, inputs_in, tail, d_hidden, out):
    d_normed = mine[...].astype(FULL) + r1[...].astype(FULL)
    d_normed = d_normed + r2[...].astype(FULL) + r3[...].astype(FULL)
    inputs = inputs_in[...].astype(FULL)
    width = inputs.shape[1]
    scale = lax.rsqrt(jnp.mean(inputs * inputs, axis=1, keepdims=True) + EPSILON)
    scaled = d_normed * tail[16:17, :]
    inner = jnp.sum(scaled * inputs, axis=1, keepdims=True) / width
    out[...] = d_hidden[...] + scaled * scale - inputs * (scale * scale * scale) * inner


def after(value, *earlier):
    return lax.optimization_barrier((value, *earlier))[0]


def along_line(block):
    return [block] + [shift(block, dz=step) for step in range(1, LINE)]


def spread(line):
    first = jnp.concatenate(line[:2], axis=0)
    second = jnp.concatenate(line[2:], axis=0)
    first = jnp.concatenate([first, shift(first, dx=1)], axis=0)
    second = jnp.concatenate([second, shift(second, dy=1)], axis=0)
    return [first, shift(first, dy=1), second, shift(second, dx=1)]


def add_low(left, right):
    return (left.astype(FULL) + right.astype(FULL)).astype(LOW)


def collect_pairs(chunks, wait=()):
    return (
        add_low(chunks[0], after(shift(chunks[1], dy=1), *wait)),
        add_low(chunks[2], after(shift(chunks[3], dx=1), *wait)),
    )


def collect_plane(pairs, wait=()):
    first, second = pairs
    half = first.shape[0] // 2
    return (
        add_low(first[:half], after(shift(first[half:], dx=1), *wait)),
        add_low(second[:half], after(shift(second[half:], dy=1), *wait)),
    )


def collect_line(planes):
    first, second = planes
    half = first.shape[0] // 2
    return [
        first[:half],
        shift(first[half:], dz=1),
        shift(second[:half], dz=2),
        shift(second[half:], dz=3),
    ]


def fast_block(
    layer_input,
    segment_ids,
    routes,
    slot_order,
    norm1_gain,
    norm2_gain,
    w_query,
    w_key,
    w_value,
    w_out,
    w_router,
    w_gate,
    w_up,
    w_down,
    cotangent,
):
    shard_index = lax.axis_index(SHARD)
    core = lax.axis_index(TENSOR)
    y_index = lax.axis_index(CONTEXT)
    z_index, x_index = shard_index // PAIR, shard_index % PAIR
    mine = x_index * PAIR + y_index
    own, width = layer_input.shape
    group = own * 2
    seq_len = segment_ids.shape[1]
    features = w_query.shape[0]
    choose = routes.shape[1]
    experts = w_router.shape[1]
    capacity = 5 * group * choose // (4 * experts)
    place = jnp.stack([z_index, shard_index * PAIR + y_index, mine]).astype(jnp.int32)

    grad_chunks = spread(along_line(cotangent))

    q_cols, k_cols = w_query.shape[1] // 4, w_key.shape[1] // 4
    extra = jnp.concatenate(
        [
            w_router,
            norm1_gain[:, None],
            norm2_gain[:, None],
            jnp.zeros((features, HEAD - 2 - experts), LOW),
        ],
        axis=1,
    )
    a_cols = q_cols + 2 * k_cols + HEAD
    packs = kernel_call(
        pack_body,
        [((features, a_cols + q_cols), LOW)] * 4,
        place,
        w_query,
        w_key,
        w_value,
        extra,
        w_out,
        scratch=[pltpu.VMEM((4, features, a_cols + q_cols), LOW)],
    )

    def exchange(blocks):
        return [
            blocks[0],
            shift(blocks[1], dy=1),
            shift(blocks[2], dx=1),
            shift(blocks[3], dx=1, dy=1),
        ]

    packs = exchange(packs)
    a_rows, b_rows = kernel_call(
        rows_body,
        [((4 * features, a_cols), LOW), ((q_cols, 4 * features), LOW)],
        place,
        *packs,
        scratch=[pltpu.VMEM((4 * features, 2 * LANES), FULL)],
    )
    a_line = along_line(a_rows)

    def gather_tokens(blocks):
        near = jnp.concatenate(blocks, axis=0)
        return near, swap_core(near)

    near_in, far_in = gather_tokens(
        [layer_input] + [after(block, a_rows) for block in plane(after(layer_input, *packs))]
    )
    near_in = after(near_in, grad_chunks[1], grad_chunks[3])
    b_line = along_line(after(b_rows, *a_line))

    def reduce_tokens(near, far):
        total = (near + far.astype(FULL)).astype(LOW)
        return exchange([total[n * own : (n + 1) * own] for n in range(4)])

    def own_first(row):
        view = row.reshape(2, 2, own)
        view = jnp.where(y_index == 0, view, view[::-1])
        view = jnp.where(core == 0, view, view[:, ::-1])
        return view.transpose(1, 0, 2).reshape(-1)

    segments = shift(segment_ids, dx=1)
    order, own_seg, other_seg, route_ids, order_ids = lax.optimization_barrier(
        (jnp.arange(seq_len, dtype=jnp.int32), segment_ids[0], segments[0], routes, slot_order[0], a_rows)
        + (grad_chunks[0], grad_chunks[2])
    )[:5]
    positions = own_first(order)
    seg_pair = jnp.stack([own_first(own_seg), own_first(other_seg)], axis=0)
    half_size = HEAD // 2
    frequency = 10000.0 ** (-jnp.arange(half_size, dtype=FULL) * 2.0 / HEAD)
    angles = positions.astype(FULL)[:, None] * frequency[None, :]
    cosine, sine = jnp.cos(angles), jnp.sin(angles)
    turns = 8
    cosine = jnp.concatenate([cosine] * turns + [jnp.ones((seq_len, LANES), FULL)], axis=1)
    sine = jnp.concatenate([-sine, sine] * (turns // 2) + [jnp.zeros((seq_len, LANES), FULL)], axis=1)

    expert_ids = jnp.arange(32, dtype=jnp.int32)
    chosen = jnp.any(route_ids[:, :, None] == expert_ids[None, None, :], axis=1)
    token_ids = jnp.arange(group, dtype=jnp.int32)
    rank = jnp.sum(
        jnp.where(order_ids[:, None] == token_ids[None, :], token_ids[:, None], 0), axis=0
    )
    own_rank = lax.dynamic_slice_in_dim(rank, core * own, own)
    own_chosen = lax.dynamic_slice_in_dim(chosen, core * own, own, 0)
    ahead = (rank[None, :] < own_rank[:, None]).astype(LOW)
    slot = dot(ahead, chosen.astype(LOW), PLAIN)
    kept = (own_chosen & (slot < capacity)).astype(FULL)
    own_chosen = own_chosen.astype(FULL)

    gate_far, up_far, down_far = swap_core(w_gate), swap_core(w_up), swap_core(w_down)
    gate_w, up_w, down_w = (
        (own_half[0], far_half[0])
        for own_half, far_half in ((w_gate, gate_far), (w_up, up_far), (w_down, down_far))
    )

    tokens = 2 * seq_len
    normed, scale_one, qkv, attended, probs, tail = kernel_call(
        attend_body,
        [
            ((tokens, width), LOW),
            ((tokens, 1), FULL),
            ((tokens, a_cols), LOW),
            ((tokens, q_cols), LOW),
            ((6, seq_len, seq_len), FULL),
            ((32, width), FULL),
        ],
        place,
        near_in,
        far_in,
        *a_line,
        cosine,
        sine,
        positions[:, None],
        positions[None, :],
        seg_pair.reshape(-1, 1),
        seg_pair,
    )
    near, far = kernel_call(
        branch_body,
        [((seq_len, width), FULL), ((seq_len, width), LOW)],
        place,
        attended,
        *b_line,
    )
    hidden_units = 2 * w_gate.shape[1]
    batch = 4 * own

    def upstream(chunk_a, chunk_b):
        return kernel_call(
            upstream_body,
            [((batch, hidden_units), FULL)] * 2 + [((batch, width), LOW)] * 2,
            place,
            chunk_a,
            chunk_b,
            *down_w,
        )

    ready = upstream(grad_chunks[0], grad_chunks[2])
    ready_far = upstream(grad_chunks[1], grad_chunks[3])
    branch = reduce_tokens(near, swap_core(far))
    branch = [branch[0]] + [after(block, *ready) for block in branch[1:]]
    hidden, mixed_ext, gates, scale_two = kernel_call(
        router_body,
        [
            ((own, width), FULL),
            ((own, width + LANES), LOW),
            ((own, 32), FULL),
            ((own, 1), FULL),
        ],
        place,
        layer_input,
        *branch,
        tail,
        own_chosen,
        kept,
    )

    half = own // 2
    first_line = along_line(mixed_ext[:half])
    second_line = along_line(after(mixed_ext[half:], *first_line))
    first_line[1:] = [after(block, *ready_far) for block in first_line[1:]]
    first, second = spread(first_line), spread(second_line)

    def expert(chunk_a, chunk_b, plain):
        return kernel_call(
            expert_body,
            [((batch // 2, width + LANES), LOW)] * 2 + [((batch, hidden_units), LOW)] * 3,
            place,
            chunk_a,
            chunk_b,
            plain,
            *gate_w,
            *up_w,
        )

    near0 = expert(first[0], first[2], ready[0])
    near1 = expert(second[0], second[2], ready[1])
    far0 = expert(after(first[1], near0[0], near1[0]), first[3], ready_far[0])
    far1 = expert(after(second[1], far0[0]), second[3], ready_far[1])
    results = (near0, far0, near1, far1)
    groups = (first[0], first[2], first[1], first[3], second[0], second[2], second[1], second[3])
    inners, d_gates, d_ups = ([result[n] for result in results] for n in (2, 3, 4))
    backs = [
        (near[0], far[0], near[1], far[1]) for near, far in (results[:2], results[2:])
    ]
    pairs0 = collect_pairs(backs[0])

    def outputs(inner0, inner1):
        return kernel_call(
            output_body,
            [((batch, width), LOW)] * 2,
            place,
            *[after(inner, *pairs0) for inner in (inner0, inner1)],
            *down_w,
        )

    out_near, out_far = outputs(inners[0], inners[2]), outputs(inners[1], inners[3])
    out_chunks = (out_near[0], out_far[0], out_near[1], out_far[1])
    pairs1 = collect_pairs(backs[1], out_chunks)
    planes0 = collect_plane(pairs0)
    planes1 = collect_plane(pairs1)
    backs = [collect_line(planes0), collect_line(planes1)]
    out_pairs = collect_pairs([after(chunk, *planes1) for chunk in out_chunks])
    d_hidden, d_branch, d_tail = kernel_call(
        middle_body,
        [((own, width), FULL), ((own, width), LOW), ((32, width), FULL)],
        place,
        *backs[0],
        *backs[1],
        tail,
        gates,
        kept,
        hidden,
        mixed_ext,
        scale_two,
        cotangent,
    )
    near, far = gather_tokens([d_branch, *plane(d_branch)])
    out_planes = collect_plane([after(pair, near, far) for pair in out_pairs])
    line_rows = 4 * features

    grad_shape = (line_rows + q_cols, a_cols)

    d_raw, d_branch_all = kernel_call(
        backward_body,
        [((tokens, a_cols), LOW), ((tokens, width), LOW)],
        place,
        near,
        far,
        *b_line,
        probs,
        qkv,
        cosine,
        sine,
        scratch=[pltpu.VMEM((tokens, a_cols), FULL)],
    )
    near, far, *line_grads = kernel_call(
        project_body,
        [((seq_len, width), FULL), ((seq_len, width), LOW), (grad_shape, FULL)]
        + [(grad_shape, LOW)] * 3,
        place,
        d_raw,
        normed,
        near_in,
        far_in,
        scale_one,
        *a_line,
        d_tail,
        d_branch_all,
        attended,
    )

    far = swap_core(far)
    d_normed = reduce_tokens(near, far)
    (grad_input,) = kernel_call(
        final_body, [((own, width), FULL)], place, *d_normed, layer_input, tail, d_hidden
    )
    shape = (3, hidden_units // 2, width)
    expert_mine, expert_send = kernel_call(
        weight_body,
        [(shape, FULL), (shape, LOW)],
        place,
        *groups,
        ready[2],
        ready_far[2],
        ready[3],
        ready_far[3],
        *[after(inner, far) for inner in inners],
        *d_gates,
        *d_ups,
    )
    expert_grads = expert_mine + swap_core(expert_send).astype(FULL)

    sums = [shift(line_grads[n], dz=n) for n in range(1, LINE)]
    out_parts = collect_line([after(block, sums[0]) for block in out_planes])
    sums = [after(block, grad_input, expert_grads) for block in sums]
    own_total, *sends = kernel_call(
        total_body,
        [((features, a_cols + q_cols), FULL)] + [((features, a_cols + q_cols), LOW)] * 3,
        place,
        line_grads[0],
        *sums,
        scratch=[pltpu.VMEM((line_rows, a_cols + 2 * LANES), FULL)],
    )
    grad_query, grad_key, grad_value, grad_out, small = kernel_call(
        gradient_body,
        [
            ((features, 4 * q_cols), FULL),
            ((features, 4 * k_cols), FULL),
            ((features, 4 * k_cols), FULL),
            ((features, 4 * q_cols), FULL),
            ((features, HEAD), LOW),
        ],
        place,
        *exchange([own_total, *sends]),
        scratch=[pltpu.VMEM((4, features, a_cols + q_cols), FULL)],
    )
    small = small.astype(FULL) + swap_core(small).astype(FULL)
    layer_output = hidden
    for block in [after(block, grad_query) for block in out_parts]:
        layer_output = layer_output + block.astype(FULL)
    layer_output = layer_output.astype(LOW)
    return (
        layer_output,
        grad_input,
        small[:, experts],
        small[:, experts + 1],
        grad_query,
        grad_key,
        grad_value,
        grad_out,
        small[:, :experts],
        expert_grads[0][None],
        expert_grads[1][None],
        expert_grads[2][None],
    )


def solution(mesh):
    in_specs = (
        P((SHARD, CONTEXT, TENSOR), None),
        P(SHARD, None),
        P(CHIPS, None),
        P(CHIPS, None),
        P(CHIPS),
        P(CHIPS),
        P(CHIPS, TENSOR),
        P(CHIPS, TENSOR),
        P(CHIPS, TENSOR),
        P(CHIPS, TENSOR),
        P(CHIPS, None),
        P(CHIPS, TENSOR, None),
        P(CHIPS, TENSOR, None),
        P(CHIPS, TENSOR, None),
        P((SHARD, CONTEXT, TENSOR), None),
    )
    out_specs = (
        P((SHARD, CONTEXT, TENSOR), None),
        P((SHARD, CONTEXT, TENSOR), None),
        P(CHIPS),
        P(CHIPS),
        P(CHIPS, TENSOR),
        P(CHIPS, TENSOR),
        P(CHIPS, TENSOR),
        P(CHIPS, TENSOR),
        P(CHIPS, None),
        P(CHIPS, TENSOR, None),
        P(CHIPS, TENSOR, None),
        P(CHIPS, TENSOR, None),
    )
    sizes = dict(mesh.shape)
    fits = (sizes[SHARD], sizes[CONTEXT], sizes[TENSOR]) == (LINE * PAIR, 2, 2)
    return jax.shard_map(
        fast_block if fits else general_block, mesh=mesh, in_specs=in_specs, out_specs=out_specs, check_vma=False
    )
```
